32 devices in a mesh: groups: 2 (over y), gx: 16 (over z, x, core).
Axes of the slice: x: 2, y: 2, z: 4, core: 2. Of those that a mesh axis runs over, the one named last changes fastest.
Arguments:
- states: float32 [2, 4, 128, 512], P(None, 'groups', 'gx'), parts along dimension 1, may hold values from -5 to 5
- pre_acts: bfloat16 [2, 3, 256, 48, 512], P(None, None, ('groups', 'gx')), parts along dimension 2, may hold values from -6 to 6
- cotangent: float32 [4, 128, 512], P('groups', 'gx'), parts along dimension 0, may hold values from -12 to 12
- weight_in: bfloat16 [9, 48, 2], replicated, may hold values from -1.5 to 1.5
- weight_second: bfloat16 [9, 48, 48], replicated, may hold values from -0.3125 to 0.3125
- weight_third: bfloat16 [9, 48, 48], replicated, may hold values from -0.3125 to 0.3125
- weight_out: bfloat16 [9, 2, 48], replicated, may hold values from -0.3125 to 0.3125
Outputs:
- state_adjoint: float32 [4, 128, 512], P('groups', 'gx'), parts along dimension 0
- grad_in: float32 [18, 48, 2], P('groups'), parts along dimension 0
- grad_second: float32 [18, 48, 48], P('groups'), parts along dimension 0
- grad_third: float32 [18, 48, 48], P('groups'), parts along dimension 0
- grad_out: float32 [18, 2, 48], P('groups'), parts along dimension 0
The draws below stay inside these ranges and needn't reach their ends.
There are 2 independent parts, one for each index of `groups`. The reference program is written for one: setup_inputs(seed, part) draws one part's arguments, and reference() takes and returns one part's arrays. A program takes and returns all parts, laid end to end along the dimension named above; an argument that names none is the same for every part. Nothing has to cross between parts.
All inputs are finite; a program needn't handle non-finite values.
Results may differ from the reference program's by a relative error of at most 0.0065.
Values may be sent and summed in bfloat16 or wider, within the bound.
No kernel may reach another device: no remote copies, remote signals or barrier semaphores. Data moves between devices by JAX's collectives and lax.ppermute only.
A program may use at most 64 MiB of HBM per device.

```python
import math
import jax
import jax.numpy as jnp

CH = 48
NY = 512
NX = 128


def draw_cotangent(key, part):
    ramp = 1.0 + 2.0 * jnp.arange(NX, dtype=jnp.float32) / (NX - 1)
    base = jnp.clip(jax.random.normal(key, (2, NX, NY), jnp.float32), -4.0, 4.0)
    return base * ramp[None, :, None]


def block_scale(key, extent, cuts, smallest, top_value):
    factor_of = 1.0
    for dim, parts in cuts:
        heights = jax.random.uniform(jax.random.fold_in(jax.random.fold_in(key, 6), dim), (parts,), jnp.float32, smallest / len(cuts), top_value / len(cuts))
        factor_of = factor_of * jnp.repeat(jnp.exp(heights), extent[dim] // parts).reshape((-1,) + (1,) * (len(extent) - 1 - dim))
    return factor_of


def gaussian(own_key, shape, deviation, most, split=(), held_as=jnp.bfloat16):
    values = deviation * jax.random.normal(own_key, shape, jnp.float32)
    if split:
        values = values * block_scale(own_key, shape, split, -0.22, 0.18)
    return jnp.clip(values, -most, most).astype(held_as)


def setup_inputs(seed: int = 0, part: int = 0) -> dict:
    splits = jax.random.split(jax.random.key(seed), 8)
    part_keys = jax.random.split(jax.random.fold_in(splits[7], part), 8)
    states = gaussian(part_keys[0], (2, 2, NX, NY), 1.0, 5.0, ((2, 16),), jnp.float32)
    pre_acts = gaussian(part_keys[1], (2, 3, NX, CH, NY), 1.0, 6.0, ((2, 16),))
    cotangent = draw_cotangent(jax.random.fold_in(jax.random.fold_in(splits[7], part), 71), part)
    weight_in = gaussian(splits[3], (9, CH, 2), 18 ** -0.5, 1.5)
    weight_second = gaussian(splits[4], (9, CH, CH), (9 * CH) ** -0.5, 0.3125)
    weight_third = gaussian(splits[5], (9, CH, CH), (9 * CH) ** -0.5, 0.3125)
    weight_out = gaussian(splits[6], (9, 2, CH), (9 * CH) ** -0.5, 0.3125)
    return {"states": states, "pre_acts": pre_acts, "cotangent": cotangent, "weight_in": weight_in, "weight_second": weight_second, "weight_third": weight_third, "weight_out": weight_out}


step_factor = 0.25
viscosity = 0.4

def pad_rows(values, rim_width):
    return jnp.concatenate([values[:, -rim_width:], values, values[:, :rim_width]], axis=1)

def pad_lead(values, rim_width):
    return jnp.concatenate([values[-rim_width:], values, values[:rim_width]], axis=0)

def half_valid(state_ext):
    row_count = state_ext.shape[1] - 2
    row_speed = state_ext[0]
    col_speed = state_ext[1][1:row_count + 1]
    face_speed = 0.25 * (row_speed[:-1] + row_speed[1:])
    side_speed = 0.25 * (col_speed + jnp.roll(col_speed, -1, axis=-1))
    outputs = []
    for component in range(2):
        values = state_ext[component]
        middle = values[1:row_count + 1]
        row_flux = face_speed * (values[:-1] + values[1:])
        col_flux = side_speed * (middle + jnp.roll(middle, -1, axis=-1))
        divergence = row_flux[1:] - row_flux[:-1] + (col_flux - jnp.roll(col_flux, 1, axis=-1))
        laplacian = values[2:] + values[:-2] + jnp.roll(middle, -1, axis=-1) + jnp.roll(middle, 1, axis=-1) - 4.0 * middle
        outputs.append(middle + step_factor * (viscosity * laplacian - divergence))
    return jnp.stack(outputs)

def relu_value(preact):
    return jnp.maximum(preact.astype(jnp.float32), jnp.float32(0.0))

def relu_slope(preact):
    return jnp.where(preact > 0, jnp.float32(1.0), jnp.float32(0.0))

def col_shifts(values):
    return [jnp.roll(values, 1, axis=-1), values, jnp.roll(values, -1, axis=-1)]

def weight_terms(gradient, source_ext):
    row_count = gradient.shape[0]
    shifted = col_shifts(source_ext)
    grad_wide = gradient.astype(jnp.float32)
    products = []
    for row_tap in range(3):
        for col_tap in range(3):
            section = shifted[col_tap][row_tap:row_tap + row_count].astype(jnp.float32)
            products.append(jnp.einsum('roy,rky->ok', grad_wide, section))
    return jnp.stack(products)

def back_conv(grad_ext, kernel):
    row_count = grad_ext.shape[0] - 2
    shifted = col_shifts(grad_ext)
    summed = None
    for row_tap in range(3):
        for col_tap in range(3):
            section = shifted[2 - col_tap][2 - row_tap:2 - row_tap + row_count].astype(jnp.float32)
            product = jnp.einsum('ok,roy->rky', kernel[3 * row_tap + col_tap].astype(jnp.float32), section)
            summed = product if summed is None else summed + product
    return summed

def backward_step(state, preacts, adjoint, kernels):
    half_value, pullback = jax.vjp(lambda values: half_valid(pad_rows(values, 1)), state)
    source_first = pad_lead(jnp.swapaxes(half_value, 0, 1).astype(jnp.bfloat16), 1)
    gradient = jnp.swapaxes(adjoint, 0, 1).astype(jnp.bfloat16)
    results = [None, None, None, None]
    backward = None
    for layer_index in (3, 2, 1, 0):
        if layer_index > 0:
            source = pad_lead(relu_value(preacts[layer_index - 1]).astype(jnp.bfloat16), 1)
        else:
            source = source_first
        results[layer_index] = weight_terms(gradient, source)
        backward = back_conv(pad_lead(gradient, 1), kernels[layer_index])
        if layer_index > 0:
            gradient = (backward * relu_slope(preacts[layer_index - 1])).astype(jnp.bfloat16)
    combined = adjoint + jnp.swapaxes(backward, 0, 1)
    return (pullback(combined)[0], results)

def reference(states, pre_acts, cotangent, weight_in, weight_second, weight_third, weight_out):
    kernels = (weight_in, weight_second, weight_third, weight_out)
    grad_totals = [jnp.zeros(kernel.shape, jnp.float32) for kernel in kernels]
    adjoint = cotangent
    for step_index in (1, 0):
        adjoint, results = backward_step(states[step_index], pre_acts[step_index], adjoint, kernels)
        grad_totals = [grad_totals[number] + results[number] for number in range(4)]
    factor = 1.0 / math.sqrt(NX * NY)
    return (adjoint, grad_totals[0] * factor, grad_totals[1] * factor, grad_totals[2] * factor, grad_totals[3] * factor)
```

```python
import functools
import math

import jax
import jax.numpy as jnp
from jax import lax
from jax.experimental import pallas as pl
from jax.experimental.pallas import tpu as pltpu
from jax.sharding import PartitionSpec as P

STEP = 0.25
VISC = 0.4
LANES = 128
BLOCK = 3
BLOCK4 = 4
SMALL = 8

F32 = jnp.float32
BF16 = jnp.bfloat16


def lane_roll(x, shift):
    width = x.shape[-1]
    return pltpu.roll(x, shift % width, x.ndim - 1)


def row_roll(x, shift):
    return pltpu.roll(x, shift % x.shape[0], 0)


def half_step(r, c):
    face = 0.25 * (r + row_roll(r, -1))
    side = 0.25 * (c + lane_roll(c, -1))
    outs = []
    for f in (r, c):
        down, right = row_roll(f, -1), lane_roll(f, -1)
        p = face * (f + down)
        q = side * (f + right)
        div = p - row_roll(p, 1) + (q - lane_roll(q, 1))
        lap = down + row_roll(f, 1) + right + lane_roll(f, 1) - 4.0 * f
        outs.append(f + STEP * (VISC * lap - div))
    return outs


def half_step_transpose(r, c, lr, lc):
    face = 0.25 * (r + row_roll(r, -1))
    side = 0.25 * (c + lane_roll(c, -1))
    outs = []
    extra_r = None
    extra_c = None
    for f, l in ((r, lr), (c, lc)):
        l_down, l_right = row_roll(l, -1), lane_roll(l, -1)
        a = STEP * (l_down - l)
        b = STEP * (l_right - l)
        ap, bq = a * face, b * side
        lap = l_down + row_roll(l, 1) + l_right + lane_roll(l, 1) - 4.0 * l
        outs.append(
            l + (STEP * VISC) * lap + (ap + row_roll(ap, 1)) + (bq + lane_roll(bq, 1))
        )
        af = a * (0.25 * (f + row_roll(f, -1)))
        bf = b * (0.25 * (f + lane_roll(f, -1)))
        extra_r = af if extra_r is None else extra_r + af
        extra_c = bf if extra_c is None else extra_c + bf
    return [
        outs[0] + (extra_r + row_roll(extra_r, 1)),
        outs[1] + (extra_c + lane_roll(extra_c, 1)),
    ]


def joined(first, own, second, even, comp):
    a, b = first[comp], second[comp]
    top = jnp.where(even, b, a)
    bottom = jnp.where(even, a, b)
    return jnp.concatenate([top, own[comp], bottom], axis=0)


def fill_small(dst, planes, rows, row0, sign):
    width = planes[0].shape[-1]
    dst[...] = jnp.zeros(dst.shape, F32)
    for comp, plane in enumerate(planes):
        value = plane.astype(BF16).astype(F32)
        for q in range(3):
            moved = value if q == 1 else lane_roll(value, sign * (q - 1))
            for i in range(rows):
                dst[SMALL * i + 2 * q + comp : SMALL * i + 2 * q + comp + 1, :] = moved[
                    row0 + i : row0 + i + 1, :
                ]


def row_conv(w_ref, src, src0, lo, hi, ch, emit):
    row = lo
    while row < hi:
        count = min(BLOCK, hi - row)
        rhs = src[(row - 1 - src0) * ch : (row + count + 1 - src0) * ch, :]
        lhs = w_ref[: count * 3 * ch, : (count + 2) * ch]
        y = jnp.dot(lhs, rhs, preferred_element_type=F32)
        for k in range(count):
            base = 3 * ch * k
            e = (
                y[base + ch : base + 2 * ch]
                + lane_roll(y[base : base + ch], -1)
                + lane_roll(y[base + 2 * ch : base + 3 * ch], 1)
            )
            emit(row + k, e)
        row += count


def chain(x4, pre, m_a, m_b, even, w4, w3, w2, d3, d2, d1, rows, ch, extra):
    e3, e2, e1 = extra
    starts = (0, e3, e3 + e2)

    def mask_rows(layer, border, row):
        if rows <= row < 2 * rows:
            return pre[layer, row - rows]
        start = starts[2 - layer]
        if row < rows:
            k = row - (rows - border)
            return jnp.where(even, m_b[start + k], m_a[start + k])
        k = row - 2 * rows
        return jnp.where(even, m_a[start + k], m_b[start + k])

    def store(dst, layer, border):
        first = rows - border

        def emit(row, e):
            a = mask_rows(layer, border, row).astype(F32)
            dst[(row - first) * ch : (row - first + 1) * ch, :] = jnp.where(
                a > 0, e, 0.0
            ).astype(BF16)

        return emit

    row, emit = rows - e3, store(d3, 2, e3)
    while row < 2 * rows + e3:
        count = min(BLOCK4, 2 * rows + e3 - row)
        rhs = x4[SMALL * (row - 1) : SMALL * (row + count + 1), :].astype(BF16)
        y = jnp.dot(
            w4[: count * ch, : SMALL * (count + 2)], rhs, preferred_element_type=F32
        )
        for k in range(count):
            emit(row + k, y[k * ch : (k + 1) * ch])
        row += count
    row_conv(w3, d3, rows - e3, rows - e2, 2 * rows + e2, ch, store(d2, 1, e2))
    row_conv(w2, d2, rows - e2, rows - e1, 2 * rows + e1, ch, store(d1, 0, e1))


def first_conv(w1, d1, src0, lo, hi, ch, emit):
    row = lo
    while row < hi:
        start = min(row, hi - BLOCK)
        rhs = d1[(start - 1 - src0) * ch : (start + BLOCK + 1 - src0) * ch, :]
        y = jnp.dot(w1[...], rhs, preferred_element_type=F32)
        e = (
            y[SMALL : 2 * SMALL]
            + lane_roll(y[:SMALL], -1)
            + lane_roll(y[2 * SMALL : 3 * SMALL], 1)
        )
        for k in range(row - start, BLOCK):
            emit(start + k, [e[2 * k + comp : 2 * k + comp + 1, :] for comp in range(2)])
        row = start + BLOCK


def weight_terms(x4, d3, d2, d1, firsts, pre, x0s, rows, ch):
    dims = (((1,), (1,)), ((), ()))

    def product(a, b):
        return lax.dot_general(a, b, dims, preferred_element_type=F32)

    def three(ref, first, row):
        return ref[(row - 1 - first) * ch : (row + 2 - first) * ch, :]

    g1 = g2 = g3 = g4 = None

    def add(total, term):
        return term if total is None else total + term

    for i in range(rows):
        row = rows + i
        source = [jnp.maximum(pre[layer, i].astype(F32), 0.0) for layer in range(3)]
        moved = [
            jnp.concatenate([lane_roll(s, 1), s, lane_roll(s, -1)], axis=0).astype(BF16)
            for s in source[:2]
        ]
        g4 = add(
            g4,
            product(
                x4[SMALL * (row - 1) : SMALL * (row + 2), :].astype(BF16),
                source[2].astype(BF16),
            ),
        )
        g3 = add(g3, product(three(d3, firsts[0], row), moved[1]))
        g2 = add(g2, product(three(d2, firsts[1], row), moved[0]))
        g1 = add(
            g1,
            product(
                three(d1, firsts[2], row),
                x0s[SMALL * i : SMALL * (i + 1), :].astype(BF16),
            ),
        )
    return g1, g2, g3, g4


def pack_rows(ch):
    return 2 * 3 * ch + 3 * ch // 2 + 3 * SMALL


def pack_terms(t_ref, terms, ch, before=None):
    g1, g2, g3, g4 = terms
    n = 3 * ch
    rest = n - LANES
    tail = jnp.concatenate([g2[:, LANES:], g3[:, LANES:], g1], axis=1)
    wide = tail.shape[1]
    half = n // 2
    parts = (
        (0, n, 0, LANES, g2[:, :LANES]),
        (n, 2 * n, 0, LANES, g3[:, :LANES]),
        (2 * n, 2 * n + half, 0, wide, tail[:half]),
        (2 * n, 2 * n + half, wide, 2 * wide, tail[half:]),
        (2 * n + half, 2 * n + half + 3 * SMALL, 0, ch, g4),
    )
    if before is None:
        t_ref[2 * n :, :] = jnp.zeros((t_ref.shape[0] - 2 * n, LANES), F32)
    else:
        t_ref[2 * n :, :] = before[2 * n :, :]
    for r0, r1, c0, c1, value in parts:
        if before is not None:
            value = value + before[r0:r1, c0:c1]
        t_ref[r0:r1, c0:c1] = value


def gather_kernel(axis, takes, rows, pre_hbm, out_a, out_b, sems):
    even = lax.rem(lax.axis_index(axis), 2) == 0
    copies = []
    for step, layer, count, dst in takes:
        low, high = 0, rows - count
        for out, start in (
            (out_a, jnp.where(even, high, low)),
            (out_b, jnp.where(even, low, high)),
        ):
            copy = pltpu.make_async_copy(
                pre_hbm.at[step, layer, pl.ds(start, count)],
                out.at[pl.ds(dst, count)],
                sems.at[len(copies)],
            )
            copy.start()
            copies.append(copy)
    for copy in copies:
        copy.wait()


def back_kernel(
    axis, rows, ch, extra,
    cot, cot_a, cot_b, pre, m_a, m_b, w4, w3, w2, w1,
    gh, x4, d3, d2, d1,
):
    even = lax.rem(lax.axis_index(axis), 2) == 0
    planes = [joined(cot_a, cot, cot_b, even, comp) for comp in range(2)]
    fill_small(x4, planes, 3 * rows, 0, 1)
    chain(x4, pre.at[0], m_a, m_b, even, w4, w3, w2, d3, d2, d1, rows, ch, extra)

    def emit(row, values):
        for comp in range(2):
            i = row - rows
            gh[comp, i : i + 1, :] = cot[comp, i : i + 1, :] + values[comp]

    first_conv(w1, d1, rows - extra[2], rows, 2 * rows, ch, emit)


def term_kernel(axis, rows, ch, extra, x4, d3, d2, d1, pre, u, u_a, u_b, t_out, x0s):
    even = lax.rem(lax.axis_index(axis), 2) == 0
    planes = [joined(u_a, u, u_b, even, comp) for comp in range(2)]
    fill_small(x0s, half_step(*planes), rows, rows, -1)
    firsts = [rows - e for e in extra]
    pack_terms(t_out, weight_terms(x4, d3, d2, d1, firsts, pre.at[0], x0s, rows, ch), ch)


def front_kernel(
    axis, rows, ch, extra,
    gh, gh_a, gh_b, u1, u1_a, u1_b, u0, u0_a, u0_b, pre, m_a, m_b, w4, w3, w2, before,
    t_out, g_out, d1, x4, d3, d2, x0s,
):
    even = lax.rem(lax.axis_index(axis), 2) == 0
    lam = [joined(gh_a, gh, gh_b, even, comp) for comp in range(2)]
    u = [joined(u1_a, u1, u1_b, even, comp) for comp in range(2)]
    planes = half_step_transpose(*u, *lam)
    for comp in range(2):
        g_out[comp] = planes[comp]
    fill_small(x4, planes, 3 * rows, 0, 1)
    u = [joined(u0_a, u0, u0_b, even, comp) for comp in range(2)]
    fill_small(x0s, half_step(*u), rows, rows, -1)
    chain(x4, pre.at[0], m_a, m_b, even, w4, w3, w2, d3, d2, d1, rows, ch, extra)
    firsts = [rows - e for e in extra]
    pack_terms(
        t_out, weight_terms(x4, d3, d2, d1, firsts, pre.at[0], x0s, rows, ch), ch, before
    )


def last_kernel(axis, rows, ch, extra, g, d1, u0, u0_a, u0_b, w1, out, gh):
    even = lax.rem(lax.axis_index(axis), 2) == 0
    for comp in range(2):
        gh[comp] = g[comp]

    def emit(row, values):
        for comp in range(2):
            gh[comp, row : row + 1, :] = g[comp, row : row + 1, :] + values[comp]

    first_conv(w1, d1, rows - extra[2], rows - 1, 2 * rows + 1, ch, emit)
    u = [joined(u0_a, u0, u0_b, even, comp) for comp in range(2)]
    planes = half_step_transpose(*u, gh[0], gh[1])
    for comp in range(2):
        out[comp] = planes[comp][rows : 2 * rows]


def unpack_kernel(axis, ch, factor, mine, other, o1, o2, o3, o4):
    even = lax.rem(lax.axis_index(axis), 2) == 0
    a, b = mine[...].astype(F32), other[...].astype(F32)
    t = factor * jnp.concatenate([jnp.where(even, a, b), jnp.where(even, b, a)], axis=0)
    n = 3 * ch
    rest = n - LANES
    half = n // 2
    wide = 2 * rest + SMALL
    low = t[2 * n : 2 * n + half]
    tail = jnp.concatenate([low[:, :wide], low[:, wide : 2 * wide]], axis=0)
    g2 = jnp.concatenate([t[:n], tail[:, :rest]], axis=1)
    g3 = jnp.concatenate([t[n : 2 * n], tail[:, rest : 2 * rest]], axis=1)
    g1 = tail[:, 2 * rest : 2 * rest + SMALL]
    g4 = t[2 * n + half : 2 * n + half + 3 * SMALL, :ch]
    for m in range(3):
        for q in range(3):
            tap = 3 * (2 - m) + q
            o2[tap] = g2[m * ch : (m + 1) * ch, q * ch : (q + 1) * ch]
            o3[tap] = g3[m * ch : (m + 1) * ch, q * ch : (q + 1) * ch]
            o1[tap] = g1[m * ch : (m + 1) * ch, 2 * q : 2 * q + 2]
            o4[tap] = g4[m * SMALL + 2 * q : m * SMALL + 2 * q + 2, :]


def band(weight, count):
    taps, o, k = weight.shape
    w = weight.reshape(3, 3, o, k)[::-1]
    w = jnp.transpose(w, (1, 3, 0, 2)).reshape(3 * k, 3 * o)
    return jnp.concatenate(
        [jnp.pad(w, ((0, 0), (b * o, (count - 1 - b) * o))) for b in range(count)], axis=0
    )


def band_last(weight, count):
    taps, o, k = weight.shape
    w = weight.reshape(3, 3, o, k)[::-1]
    w = jnp.transpose(w, (3, 0, 1, 2)).reshape(k, 3, 3 * o)
    w = jnp.pad(w, ((0, 0), (0, 0), (0, SMALL - 3 * o))).reshape(k, 3 * SMALL)
    return jnp.concatenate(
        [jnp.pad(w, ((0, 0), (b * SMALL, (count - 1 - b) * SMALL))) for b in range(count)],
        axis=0,
    )


def band_first(weight, count):
    taps, o, k = weight.shape
    w = weight.reshape(3, 3, o, k)[::-1]
    w = jnp.transpose(w, (1, 3, 0, 2)).reshape(3, k, 3 * o)
    w = jnp.concatenate(
        [
            jnp.pad(w, ((0, 0), (0, 0), (b * o, (count - 1 - b) * o)))
            for b in range(count)
        ],
        axis=1,
    )
    w = jnp.pad(w, ((0, 0), (0, SMALL - count * k), (0, 0)))
    return w.reshape(3 * SMALL, (count + 2) * o)


VMEM = pl.BlockSpec(memory_space=pltpu.VMEM)


def call(kernel, outs, scratch, args, specs=None, limit=24 << 20, flops=10**8):
    specs = specs or {}
    return pl.pallas_call(
        kernel,
        out_shape=outs,
        grid=(1,) if specs else (),
        in_specs=[specs.get(i, VMEM) for i in range(len(args))],
        out_specs=jax.tree.map(lambda _: VMEM, outs),
        scratch_shapes=scratch,
        compiler_params=pltpu.CompilerParams(vmem_limit_bytes=limit),
        cost_estimate=pl.CostEstimate(
            flops=flops, bytes_accessed=2 * 10**6, transcendentals=0
        ),
    )(*args)


def on_device(states, pre_acts, cotangent, weight_in, weight_second, weight_third, weight_out):
    axis = "gx"
    count = lax.axis_size(axis)
    _, _, rows, width = states.shape
    ch = pre_acts.shape[3]

    pair_a = [(i, i ^ 1) for i in range(count)]
    pair_b = [(i, (i + 1) % count if i % 2 else (i - 1) % count) for i in range(count)]

    def swap(for_a, for_b):
        return lax.ppermute(for_a, axis, pair_a), lax.ppermute(for_b, axis, pair_b)

    def shape(*dims, dtype=F32):
        return jax.ShapeDtypeStruct(dims, dtype)

    back_extra, front_extra = (3, 2, 1), (4, 3, 2)

    def borders(step, extra):
        takes, total = [], 0
        for layer, border in zip((2, 1, 0), extra):
            takes.append((step, layer, border, total))
            total += border
        out = shape(total, ch, width, dtype=BF16)
        return pl.pallas_call(
            functools.partial(gather_kernel, axis, takes, rows),
            out_shape=[out, out],
            in_specs=[pl.BlockSpec(memory_space=pl.ANY)],
            out_specs=[VMEM, VMEM],
            scratch_shapes=[pltpu.SemaphoreType.DMA((2 * len(takes),))],
            compiler_params=pltpu.CompilerParams(vmem_limit_bytes=8 << 20),
        )(pre_acts)

    cot_a, cot_b = swap(cotangent, cotangent)
    m1_a, m1_b = swap(*borders(1, back_extra))
    u_all = states.reshape((-1,) + states.shape[2:])
    u_a, u_b = swap(u_all, u_all)
    m0_a, m0_b = swap(*borders(0, front_extra))
    u1, u1_a, u1_b = states[1], u_a[2:], u_b[2:]
    u0, u0_a, u0_b = states[0], u_a[:2], u_b[:2]

    w4 = band_last(weight_out, BLOCK4)
    w3 = band(weight_third, BLOCK)
    w2 = band(weight_second, BLOCK)
    w1 = band_first(weight_in, BLOCK)

    def pre_spec(step):
        return pl.BlockSpec(
            (1,) + pre_acts.shape[1:], lambda *_: (step, 0, 0, 0, 0)
        )

    def d_shapes(extra):
        return [shape((rows + 2 * e) * ch, width, dtype=BF16) for e in extra]

    x4_shape = shape(3 * rows * SMALL, width)
    gh, x4, d3, d2, d1 = call(
        functools.partial(back_kernel, axis, rows, ch, back_extra),
        [shape(2, rows, width), x4_shape] + d_shapes(back_extra),
        [],
        (cotangent, cot_a, cot_b, pre_acts, m1_a, m1_b, w4, w3, w2, w1),
        {3: pre_spec(1)},
    )
    gh_a, gh_b = swap(gh, gh)
    x0s = pltpu.VMEM((rows * SMALL, width), F32)
    before = call(
        functools.partial(term_kernel, axis, rows, ch, back_extra),
        shape(pack_rows(ch), LANES),
        [x0s],
        (x4, d3, d2, d1, pre_acts, u1, u1_a, u1_b),
        {4: pre_spec(1)},
    )
    front_d = d_shapes(front_extra)
    total, g, d1 = call(
        functools.partial(front_kernel, axis, rows, ch, front_extra),
        [shape(pack_rows(ch), LANES), shape(2, 3 * rows, width), front_d[2]],
        [pltpu.VMEM(x4_shape.shape, F32)]
        + [pltpu.VMEM(s.shape, s.dtype) for s in front_d[:2]]
        + [x0s],
        (gh, gh_a, gh_b, u1, u1_a, u1_b, u0, u0_a, u0_b, pre_acts, m0_a, m0_b, w4, w3, w2, before),
        {9: pre_spec(0)},
    )
    adjoint = call(
        functools.partial(last_kernel, axis, rows, ch, front_extra),
        shape(2, rows, width),
        [pltpu.VMEM((2, 3 * rows, width), F32)],
        (g, d1, u0, u0_a, u0_b, w1),
    )

    side = lax.rem(lax.axis_index(axis), 2)
    half = total.shape[0] // 2
    keep = lax.dynamic_slice_in_dim(total, side * half, half, 0)
    give = lax.dynamic_slice_in_dim(total, (1 - side) * half, half, 0)
    mine = keep + lax.ppermute(give, axis, pair_a)
    bit = 2
    while bit < count:
        others = [bit] if bit == 2 or 2 * bit >= count else [bit, 2 * bit, 3 * bit]
        got = [
            lax.ppermute(mine, axis, [(i, i ^ b) for i in range(count)]) for b in others
        ]
        if len(others) == 1:
            mine = mine + got[0]
            bit *= 2
        else:
            mine = (mine + got[0]) + (got[1] + got[2])
            bit *= 4
    other = lax.ppermute(mine, axis, pair_a)
    factor = 1.0 / math.sqrt(rows * count * width)
    g1, g2, g3, g4 = call(
        functools.partial(unpack_kernel, axis, ch, factor),
        [shape(*w.shape) for w in (weight_in, weight_second, weight_third, weight_out)],
        [],
        (mine, other),
    )
    return adjoint, g1, g2, g3, g4


def solution(mesh):
    return jax.shard_map(
        on_device,
        mesh=mesh,
        in_specs=(
            P(None, "groups", "gx", None),
            P(None, None, ("groups", "gx"), None, None),
            P("groups", "gx", None),
            P(),
            P(),
            P(),
            P(),
        ),
        out_specs=(
            P("groups", "gx", None),
            P("groups", None, None),
            P("groups", None, None),
            P("groups", None, None),
            P("groups", None, None),
        ),
        check_vma=False,
    )
```

```python
import functools
import math

import jax
import jax.numpy as jnp
from jax import lax
from jax.experimental import pallas as pl
from jax.experimental.pallas import tpu as pltpu
from jax.sharding import PartitionSpec as P


STEP = 0.25
VISC = 0.4
LANES = 128
BLOCK = 3
BLOCK4 = 4
VMEM_BYTES = 67043328
BORDERS = (2, 1, 0)
EMPTY = 2
SMALL = 8

F32 = jnp.float32
BF16 = jnp.bfloat16


def lane_roll(x, shift):
    width = x.shape[-1]
    return pltpu.roll(x, shift % width, x.ndim - 1)


def row_roll(x, shift):
    return pltpu.roll(x, shift % x.shape[0], 0)


def half_step(r, c):
    face = 0.25 * (r + row_roll(r, -1))
    side = 0.25 * (c + lane_roll(c, -1))
    outs = []
    for f in (r, c):
        down, right = row_roll(f, -1), lane_roll(f, -1)
        p = face * (f + down)
        q = side * (f + right)
        div = p - row_roll(p, 1) + (q - lane_roll(q, 1))
        lap = down + row_roll(f, 1) + right + lane_roll(f, 1) - 4.0 * f
        outs.append(f + STEP * (VISC * lap - div))
    return outs


def half_step_transpose(r, c, lr, lc):
    face = 0.25 * (r + row_roll(r, -1))
    side = 0.25 * (c + lane_roll(c, -1))
    outs = []
    extra_r = None
    extra_c = None
    for f, l in ((r, lr), (c, lc)):
        l_down, l_right = row_roll(l, -1), lane_roll(l, -1)
        a = STEP * (l_down - l)
        b = STEP * (l_right - l)
        ap, bq = a * face, b * side
        lap = l_down + row_roll(l, 1) + l_right + lane_roll(l, 1) - 4.0 * l
        outs.append(
            l + (STEP * VISC) * lap + (ap + row_roll(ap, 1)) + (bq + lane_roll(bq, 1))
        )
        af = a * (0.25 * (f + row_roll(f, -1)))
        bf = b * (0.25 * (f + lane_roll(f, -1)))
        extra_r = af if extra_r is None else extra_r + af
        extra_c = bf if extra_c is None else extra_c + bf
    return [
        outs[0] + (extra_r + row_roll(extra_r, 1)),
        outs[1] + (extra_c + lane_roll(extra_c, 1)),
    ]


def joined(a, own, b, even):
    return jnp.concatenate([jnp.where(even, b, a), own, jnp.where(even, a, b)], axis=0)


def split_terms(x):
    high = x.astype(BF16).astype(F32)
    return jnp.concatenate([high, x - high], axis=0).astype(BF16)


def border_planes(ref, first, rows, count):
    parts = [
        ref[first + 2 * rows * i : first + 2 * rows * (i + 1), :].astype(F32)
        for i in range(count)
    ]
    return [p[:rows] + p[rows:] for p in parts]


def fill_small(dst, planes, rows, row0, sign):
    dst[...] = jnp.zeros(dst.shape, F32)
    for comp, plane in enumerate(planes):
        value = plane.astype(BF16).astype(F32)
        for q in range(3):
            moved = value if q == 1 else lane_roll(value, sign * (q - 1))
            for i in range(rows):
                dst[SMALL * i + 2 * q + comp : SMALL * i + 2 * q + comp + 1, :] = moved[
                    row0 + i : row0 + i + 1, :
                ]


def row_conv(w_ref, src, src0, lo, hi, ch, emit):
    row = lo
    while row < hi:
        count = min(BLOCK, hi - row)
        rhs = src[(row - 1 - src0) * ch : (row + count + 1 - src0) * ch, :]
        lhs = w_ref[: count * 3 * ch, : (count + 2) * ch]
        y = jnp.dot(lhs, rhs, preferred_element_type=F32)
        for k in range(count):
            base = 3 * ch * k
            e = (
                y[base + ch : base + 2 * ch]
                + lane_roll(y[base : base + ch], -1)
                + lane_roll(y[base + 2 * ch : base + 3 * ch], 1)
            )
            emit(row + k, e)
        row += count


def chain(x4, pre, m_a, m_b, even, w4, w3, w2, d3, d2, d1, rows, ch):
    e3, e2, e1 = BORDERS

    def mask_rows(layer, row):
        if rows <= row < 2 * rows:
            return pre[layer, row - rows].astype(F32)
        above = row < rows
        border, start = ((e1, e3 + e2), (e2, e3), (e3, 0))[layer]
        k = start + (row - (rows - border) if above else row - 2 * rows)
        a, b = (m[k * ch : (k + 1) * ch, :].astype(F32) for m in (m_a, m_b))
        return jnp.where(even, b, a) if above else jnp.where(even, a, b)

    def store(dst, layer, first):
        def emit(row, e):
            dst[(row - first) * ch : (row - first + 1) * ch, :] = jnp.where(
                mask_rows(layer, row) > 0, e, 0.0
            ).astype(BF16)

        return emit

    row, emit = rows - e3, store(d3, 2, rows - e3)
    while row < 2 * rows + e3:
        count = min(BLOCK4, 2 * rows + e3 - row)
        rhs = x4[SMALL * (row - 1) : SMALL * (row + count + 1), :].astype(BF16)
        y = jnp.dot(
            w4[: count * ch, : SMALL * (count + 2)], rhs, preferred_element_type=F32
        )
        for k in range(count):
            emit(row + k, y[k * ch : (k + 1) * ch])
        row += count
    row_conv(w3, d3, rows - e3, rows - e2, 2 * rows + e2, ch, store(d2, 1, rows - e2))
    empty = jnp.zeros((EMPTY * ch, d1.shape[-1]), BF16)
    d1[: EMPTY * ch, :] = empty
    d1[(rows + EMPTY) * ch :, :] = empty
    row_conv(w2, d2, rows - e2, rows, 2 * rows, ch, store(d1, 0, rows - EMPTY))


def first_conv(w1, d1, src0, lo, hi, ch, emit):
    row = lo
    while row < hi:
        start = min(row, hi - BLOCK)
        rhs = d1[(start - 1 - src0) * ch : (start + BLOCK + 1 - src0) * ch, :]
        y = jnp.dot(w1[...], rhs, preferred_element_type=F32)
        e = (
            y[SMALL : 2 * SMALL]
            + lane_roll(y[:SMALL], -1)
            + lane_roll(y[2 * SMALL : 3 * SMALL], 1)
        )
        for k in range(row - start, BLOCK):
            emit(start + k, [e[2 * k + comp : 2 * k + comp + 1, :] for comp in range(2)])
        row = start + BLOCK


def weight_terms(x4, d3, d2, d1, pre, x0s, rows, ch):
    dims = (((1,), (1,)), ((), ()))

    def product(a, b):
        return lax.dot_general(a, b, dims, preferred_element_type=F32)

    def three(ref, row, border):
        row -= rows - border
        return ref[(row - 1) * ch : (row + 2) * ch, :]

    totals = [None] * 4
    for i in range(rows):
        row = rows + i
        source = [jnp.maximum(pre[layer, i].astype(F32), 0.0) for layer in range(3)]
        moved = [
            jnp.concatenate([lane_roll(s, 1), s, lane_roll(s, -1)], axis=0).astype(BF16)
            for s in source[:2]
        ]
        terms = (
            product(
                x0s[SMALL * i : SMALL * (i + 3), :].astype(BF16),
                d1[(i + EMPTY) * ch : (i + EMPTY + 1) * ch, :],
            ),
            product(three(d2, row, BORDERS[1]), moved[0]),
            product(three(d3, row, BORDERS[0]), moved[1]),
            product(
                x4[SMALL * (row - 1) : SMALL * (row + 2), :].astype(BF16),
                source[2].astype(BF16),
            ),
        )
        totals = [t if old is None else old + t for old, t in zip(totals, terms)]
    return totals


def pack_rows(ch):
    n = 3 * ch
    return -(-(2 * n + n // 2 + 3 * SMALL) // 32) * 32


def pack_terms(t_ref, terms, ch, before=None):
    g1, g2, g3, g4 = terms
    n = 3 * ch
    low = 2 * n + n // 2
    tail = jnp.concatenate([g2[:, LANES:], g3[:, LANES:]], axis=1)
    wide = tail.shape[1]
    parts = (
        (0, n, 0, LANES, g2[:, :LANES]),
        (n, 2 * n, 0, LANES, g3[:, :LANES]),
        (2 * n, low, 0, wide, tail[: n // 2]),
        (2 * n, low, wide, 2 * wide, tail[n // 2 :]),
        (low, low + 3 * SMALL, 0, 2 * ch, jnp.concatenate([g4, g1], axis=1)),
    )
    t_ref[2 * n :, :] = jnp.zeros((t_ref.shape[0] - 2 * n, LANES), F32)
    for r0, r1, c0, c1, value in parts:
        if before is not None:
            value = value + before[r0:r1, c0:c1]
        t_ref[r0:r1, c0:c1] = value


def border_copies(axis, takes, rows, ch, pre_hbm, out_a, out_b, sems):
    even = lax.rem(lax.axis_index(axis), 2) == 0
    copies = []
    for step, layer, count, dst in takes:
        low, high = 0, (rows - count) * ch
        for out, start in (
            (out_a, jnp.where(even, high, low)),
            (out_b, jnp.where(even, low, high)),
        ):
            copy = pltpu.make_async_copy(
                pre_hbm.at[step, layer, pl.ds(pl.multiple_of(start, ch), count * ch)],
                out.at[pl.ds(dst * ch, count * ch)],
                sems.at[len(copies)],
            )
            copy.start()
            copies.append(copy)
    return copies


def gather_kernel(axis, takes, rows, ch, base, step, with_d4, pre_hbm, states, cot, out_a, out_b, sems):
    copies = border_copies(axis, takes, rows, ch, pre_hbm, out_a, out_b, sems)
    planes = [split_terms(states[step, comp]) for comp in range(2)]
    if with_d4:
        planes.append(jnp.concatenate([cot[0], cot[1]], axis=0).astype(BF16))
    for i, plane in enumerate(planes):
        for out in (out_a, out_b):
            out[base + 2 * rows * i : base + 2 * rows * (i + 1), :] = plane
    for copy in copies:
        copy.wait()


def weights_kernel(ch, w1, w2, w3, w4, o1, o2, o3, o4):
    for w, o in ((w3, o3), (w2, o2)):
        for q in range(3):
            block = jnp.concatenate([w[3 * (2 - m) + q].astype(F32) for m in range(3)], axis=0)
            block = block.T.astype(BF16)
            for b in range(BLOCK):
                r = (3 * b + q) * ch
                o[r : r + ch, :] = placed(block, b * ch, o.shape[1])
    zero = jnp.zeros((SMALL - 6, ch), F32)
    block = jnp.concatenate(
        [
            piece
            for m in range(3)
            for piece in [w4[3 * (2 - m) + q].astype(F32) for q in range(3)] + [zero]
        ],
        axis=0,
    )
    block = block.T.astype(BF16)
    for b in range(BLOCK4):
        o4[b * ch : (b + 1) * ch, :] = placed(block, b * SMALL, o4.shape[1])
    rows = []
    for q in range(3):
        block = jnp.concatenate([w1[3 * (2 - m) + q].astype(F32) for m in range(3)], axis=1)
        for b in range(BLOCK):
            rows.append(placed(block, b * ch, o1.shape[1]))
        rows.append(jnp.zeros((SMALL - 2 * BLOCK, o1.shape[1]), F32))
    o1[...] = jnp.concatenate(rows, axis=0).astype(BF16)


def placed(block, column, width):
    parts = [block]
    if column:
        parts.insert(0, jnp.zeros((block.shape[0], column), block.dtype))
    rest = width - column - block.shape[1]
    if rest:
        parts.append(jnp.zeros((block.shape[0], rest), block.dtype))
    return jnp.concatenate(parts, axis=1)


def partial_input(w1, d1, own, out, rows, ch):
    out[2 * rows :, :] = jnp.zeros((SMALL, out.shape[1]), F32)

    def emit(row, values):
        i = row - rows
        for comp in range(2):
            if 0 <= i < rows:
                k = rows * comp + i
                out[k : k + 1, :] = own(comp, i) + values[comp]
            else:
                k = 2 * rows + 2 * comp + (i > 0)
                out[k : k + 1, :] = values[comp]

    first_conv(w1, d1, rows - EMPTY, rows - 1, 2 * rows + 1, ch, emit)


def whole_input(gh, gh_a, gh_b, lam, rows, even):
    a, b = gh_a[...], gh_b[...]
    above, below = jnp.where(even, b, a), jnp.where(even, a, b)
    for comp in range(2):
        own = slice(rows * comp, rows * (comp + 1))
        lam[comp, :rows, :] = above[own]
        lam[comp, rows : 2 * rows, :] = gh[own, :]
        lam[comp, 2 * rows :, :] = below[own]
        k = 2 * rows + 2 * comp
        for row, part in (
            (rows - 1, gh[k : k + 1, :]),
            (rows, above[k + 1 : k + 2]),
            (2 * rows - 1, below[k : k + 1]),
            (2 * rows, gh[k + 1 : k + 2, :]),
        ):
            lam[comp, row : row + 1, :] += part


def border_states(states, step, m_a, m_b, rows, ch, even):
    a = border_planes(m_a, sum(BORDERS) * ch, rows, 2)
    b = border_planes(m_b, sum(BORDERS) * ch, rows, 2)
    return [joined(a[comp], states[step, comp], b[comp], even) for comp in range(2)]


def back_kernel(axis, rows, ch, cot, pre, m_a, m_b, w4, w3, w2, w1, gh, x4, d3, d2, d1):
    even = lax.rem(lax.axis_index(axis), 2) == 0
    base = sum(BORDERS) * ch + 4 * rows
    a, b = (m[base : base + 2 * rows, :].astype(F32) for m in (m_a, m_b))
    planes = [
        joined(
            a[rows * comp : rows * (comp + 1)], cot[comp], b[rows * comp : rows * (comp + 1)], even
        )
        for comp in range(2)
    ]
    fill_small(x4, planes, 3 * rows, 0, 1)
    chain(x4, pre.at[0], m_a, m_b, even, w4, w3, w2, d3, d2, d1, rows, ch)
    partial_input(w1, d1, lambda comp, i: cot[comp, i : i + 1, :], gh, rows, ch)


def term_kernel(axis, rows, ch, x4, d3, d2, d1, pre, states, m_a, m_b, t_out, u_out, x0s):
    even = lax.rem(lax.axis_index(axis), 2) == 0
    u = border_states(states, 1, m_a, m_b, rows, ch, even)
    for comp in range(2):
        u_out[comp] = u[comp]
    fill_small(x0s, half_step(*u), rows + 2, rows - 1, -1)
    pack_terms(t_out, weight_terms(x4, d3, d2, d1, pre.at[0], x0s, rows, ch), ch)


def front_kernel(
    axis, rows, ch,
    gh, gh_a, gh_b, u1, states, pre, m_a, m_b, w4, w3, w2, before,
    keep, give, g_out, u_out, d1, x4, d3, d2, x0s, total, lam,
):
    even = lax.rem(lax.axis_index(axis), 2) == 0
    whole_input(gh, gh_a, gh_b, lam, rows, even)
    planes = half_step_transpose(u1[0], u1[1], lam[0], lam[1])
    for comp in range(2):
        g_out[comp] = planes[comp][rows : 2 * rows]
    fill_small(x4, planes, 3 * rows, 0, 1)
    u = border_states(states, 0, m_a, m_b, rows, ch, even)
    for comp in range(2):
        u_out[comp] = u[comp]
    fill_small(x0s, half_step(*u), rows + 2, rows - 1, -1)
    chain(x4, pre.at[0], m_a, m_b, even, w4, w3, w2, d3, d2, d1, rows, ch)
    pack_terms(total, weight_terms(x4, d3, d2, d1, pre.at[0], x0s, rows, ch), ch, before)
    half = total.shape[0] // 2
    a, b = total[:half, :], total[half:, :]
    keep[...] = jnp.where(even, a, b)
    give[...] = jnp.where(even, b, a)


def input_kernel(rows, ch, g, d1, w1, gh):
    partial_input(w1, d1, lambda comp, i: g[comp, i : i + 1, :], gh, rows, ch)


def last_kernel(axis, rows, gh, gh_a, gh_b, u, out, lam):
    even = lax.rem(lax.axis_index(axis), 2) == 0
    whole_input(gh, gh_a, gh_b, lam, rows, even)
    planes = half_step_transpose(u[0], u[1], lam[0], lam[1])
    for comp in range(2):
        out[comp] = planes[comp][rows : 2 * rows]


def unpack_kernel(axis, ch, factor, mine, other, o1, o2, o3, o4):
    even = lax.rem(lax.axis_index(axis), 2) == 0
    a, b = mine[...].astype(F32), other[...].astype(F32)
    t = factor * jnp.concatenate([jnp.where(even, a, b), jnp.where(even, b, a)], axis=0)
    n = 3 * ch
    rest = n - LANES
    wide = 2 * rest
    low = 2 * n + n // 2
    tail = t[2 * n : low]
    tail = jnp.concatenate([tail[:, :wide], tail[:, wide : 2 * wide]], axis=0)
    g2 = jnp.concatenate([t[:n], tail[:, :rest]], axis=1)
    g3 = jnp.concatenate([t[n : 2 * n], tail[:, rest:]], axis=1)
    g4 = t[low : low + 3 * SMALL, :ch]
    g1 = t[low : low + 3 * SMALL, ch : 2 * ch]
    for m in range(3):
        for q in range(3):
            tap = 3 * (2 - m) + q
            o2[tap] = g2[m * ch : (m + 1) * ch, q * ch : (q + 1) * ch]
            o3[tap] = g3[m * ch : (m + 1) * ch, q * ch : (q + 1) * ch]
            small = slice(m * SMALL + 2 * q, m * SMALL + 2 * q + 2)
            o4[tap] = g4[small]
            o1[3 * m + q] = g1[small]


VMEM = pl.BlockSpec(memory_space=pltpu.VMEM)


def call(kernel, outs, scratch, args, specs=None, limit=24 << 20, flops=10**8):
    specs = specs or {}
    return pl.pallas_call(
        kernel,
        out_shape=outs,
        grid=(1,) if specs else (),
        in_specs=[specs.get(i, VMEM) for i in range(len(args))],
        out_specs=jax.tree.map(lambda _: VMEM, outs),
        scratch_shapes=scratch,
        compiler_params=pltpu.CompilerParams(vmem_limit_bytes=limit),
        cost_estimate=pl.CostEstimate(
            flops=flops, bytes_accessed=2 * 10**6, transcendentals=0
        ),
    )(*args)


def on_device(states, pre_acts, cotangent, weight_in, weight_second, weight_third, weight_out):
    axis = "gx"
    count = lax.axis_size(axis)
    _, _, rows, width = states.shape
    ch = pre_acts.shape[3]
    flat = pre_acts.reshape(pre_acts.shape[:2] + (rows * ch, width))

    pair_a = [(i, i ^ 1) for i in range(count)]
    pair_b = [(i, (i + 1) % count if i % 2 else (i - 1) % count) for i in range(count)]

    def swap(for_a, for_b):
        b = lax.ppermute(for_b, axis, pair_b)
        a = lax.ppermute(for_a, axis, pair_a)
        return a, b

    def shape(*dims, dtype=F32):
        return jax.ShapeDtypeStruct(dims, dtype)

    def borders(step, with_d4, room):
        takes, total = [], 0
        for layer, border in zip((2, 1, 0), BORDERS):
            if not border:
                continue
            takes.append((step, layer, border, total))
            total += border
        base = total * ch
        out = shape(base + (6 if with_d4 else 4) * rows, width, dtype=BF16)
        pack = pl.pallas_call(
            functools.partial(gather_kernel, axis, takes, rows, ch, base, step, with_d4),
            out_shape=[out, out],
            in_specs=[pl.BlockSpec(memory_space=pltpu.HBM), VMEM, VMEM],
            out_specs=[VMEM, VMEM],
            scratch_shapes=[pltpu.SemaphoreType.DMA((2 * len(takes),))],
            compiler_params=pltpu.CompilerParams(vmem_limit_bytes=VMEM_BYTES - room),
        )
        a, b = pack(flat, states, cotangent)
        return swap(a, b)

    m1_a, m1_b = borders(1, True, 3 << 20)
    m0_a, m0_b = borders(0, False, 56 << 20)

    def bands(n, m):
        return shape(n, m, dtype=BF16)

    w1, w2, w3, w4 = call(
        functools.partial(weights_kernel, ch),
        [
            bands(3 * SMALL, (BLOCK + 2) * ch),
            bands(3 * BLOCK * ch, (BLOCK + 2) * ch),
            bands(3 * BLOCK * ch, (BLOCK + 2) * ch),
            bands(BLOCK4 * ch, (BLOCK4 + 2) * SMALL),
        ],
        [],
        (jnp.swapaxes(weight_in, 1, 2), weight_second, weight_third, weight_out),
    )

    def pre_spec(step):
        return pl.BlockSpec((1,) + pre_acts.shape[1:], lambda *_: (step, 0, 0, 0, 0))

    def d_shape(border):
        return shape((rows + 2 * border) * ch, width, dtype=BF16)

    def scratch(*shapes):
        return [pltpu.VMEM(s.shape, s.dtype) for s in shapes]

    x4_shape = shape(3 * rows * SMALL, width)
    x0_shape = shape((rows + 2) * SMALL, width)
    d_shapes = [d_shape(BORDERS[0]), d_shape(BORDERS[1]), d_shape(EMPTY)]
    planes = shape(2, 3 * rows, width)
    part = shape(2 * rows + SMALL, width)
    total = shape(pack_rows(ch), LANES)
    half = shape(pack_rows(ch) // 2, LANES)
    gh, x4, d3, d2, d1 = call(
        functools.partial(back_kernel, axis, rows, ch),
        [part, x4_shape] + d_shapes,
        [],
        (cotangent, pre_acts, m1_a, m1_b, w4, w3, w2, w1),
        {1: pre_spec(1)},
    )
    gh_a, gh_b = swap(gh, gh)
    before, u1 = call(
        functools.partial(term_kernel, axis, rows, ch),
        [total, planes],
        scratch(x0_shape),
        (x4, d3, d2, d1, pre_acts, states, m1_a, m1_b),
        {4: pre_spec(1)},
    )
    keep, give, g, u0, d1 = call(
        functools.partial(front_kernel, axis, rows, ch),
        [half, half, shape(2, rows, width), planes, d_shapes[2]],
        scratch(x4_shape, d_shapes[0], d_shapes[1], x0_shape, total, planes),
        (gh, gh_a, gh_b, u1, states, pre_acts, m0_a, m0_b, w4, w3, w2, before),
        {5: pre_spec(0)},
    )
    gh0 = call(functools.partial(input_kernel, rows, ch), part, [], (g, d1, w1))
    gh0_a, gh0_b = swap(gh0, gh0)
    adjoint = call(
        functools.partial(last_kernel, axis, rows),
        shape(2, rows, width),
        scratch(planes),
        (gh0, gh0_a, gh0_b, u0),
    )

    mine = keep + lax.ppermute(give, axis, pair_a)
    bit = 2
    while bit < count:
        mine = mine.astype(BF16)
        got = lax.ppermute(mine, axis, [(i, i ^ bit) for i in range(count)])
        if 2 * bit >= count:
            got, adjoint = lax.optimization_barrier((got, adjoint))
        mine = mine.astype(F32) + got.astype(F32)
        bit *= 2
    other = lax.ppermute(mine, axis, pair_a)
    factor = 1.0 / math.sqrt(rows * count * width)
    g1, g2, g3, g4 = call(
        functools.partial(unpack_kernel, axis, ch, factor),
        [
            shape(*w)
            for w in (
                weight_out.shape[:1] + (weight_in.shape[2], ch),
                weight_second.shape,
                weight_third.shape,
                weight_out.shape,
            )
        ],
        [],
        (mine, other),
    )
    return adjoint, jnp.swapaxes(g1, 1, 2), g2, g3, g4


def solution(mesh):
    return jax.shard_map(
        on_device,
        mesh=mesh,
        in_specs=(
            P(None, "groups", "gx", None),
            P(None, None, ("groups", "gx"), None, None),
            P("groups", "gx", None),
            P(),
            P(),
            P(),
            P(),
        ),
        out_specs=(
            P("groups", "gx", None),
            P("groups", None, None),
            P("groups", None, None),
            P("groups", None, None),
            P("groups", None, None),
        ),
        check_vma=False,
    )
```

```python
import functools
import math

import jax
import jax.numpy as jnp
from jax import lax
from jax.experimental import pallas as pl
from jax.experimental.pallas import tpu as pltpu
from jax.sharding import PartitionSpec as P


STEP = 0.25
VISC = 0.4
LANES = 128
BLOCK = 3
BLOCK4 = 4
VMEM_BYTES = 67043328
BORDERS = (2, 1, 0)
EMPTY = 2
SMALL = 8

F32 = jnp.float32
BF16 = jnp.bfloat16


def lane_roll(x, shift):
    width = x.shape[-1]
    return pltpu.roll(x, shift % width, x.ndim - 1)


def row_roll(x, shift):
    return pltpu.roll(x, shift % x.shape[0], 0)


def half_step(r, c):
    face = 0.25 * (r + row_roll(r, -1))
    side = 0.25 * (c + lane_roll(c, -1))
    outs = []
    for f in (r, c):
        down, right = row_roll(f, -1), lane_roll(f, -1)
        p = face * (f + down)
        q = side * (f + right)
        div = p - row_roll(p, 1) + (q - lane_roll(q, 1))
        lap = down + row_roll(f, 1) + right + lane_roll(f, 1) - 4.0 * f
        outs.append(f + STEP * (VISC * lap - div))
    return outs


def half_step_transpose(r, c, lr, lc):
    face = 0.25 * (r + row_roll(r, -1))
    side = 0.25 * (c + lane_roll(c, -1))
    outs = []
    extra_r = None
    extra_c = None
    for f, l in ((r, lr), (c, lc)):
        l_down, l_right = row_roll(l, -1), lane_roll(l, -1)
        a = STEP * (l_down - l)
        b = STEP * (l_right - l)
        ap, bq = a * face, b * side
        lap = l_down + row_roll(l, 1) + l_right + lane_roll(l, 1) - 4.0 * l
        outs.append(
            l + (STEP * VISC) * lap + (ap + row_roll(ap, 1)) + (bq + lane_roll(bq, 1))
        )
        af = a * (0.25 * (f + row_roll(f, -1)))
        bf = b * (0.25 * (f + lane_roll(f, -1)))
        extra_r = af if extra_r is None else extra_r + af
        extra_c = bf if extra_c is None else extra_c + bf
    return [
        outs[0] + (extra_r + row_roll(extra_r, 1)),
        outs[1] + (extra_c + lane_roll(extra_c, 1)),
    ]


def joined(a, own, b, even):
    return jnp.concatenate([jnp.where(even, b, a), own, jnp.where(even, a, b)], axis=0)


def split_terms(x):
    high = x.astype(BF16).astype(F32)
    return jnp.concatenate([high, x - high], axis=0).astype(BF16)


def border_planes(ref, first, rows, count):
    parts = [
        ref[first + 2 * rows * i : first + 2 * rows * (i + 1), :].astype(F32)
        for i in range(count)
    ]
    return [p[:rows] + p[rows:] for p in parts]


def fill_small(dst, planes, rows, row0, sign):
    dst[...] = jnp.zeros(dst.shape, F32)
    for comp, plane in enumerate(planes):
        value = plane.astype(BF16).astype(F32)
        for q in range(3):
            moved = value if q == 1 else lane_roll(value, sign * (q - 1))
            for i in range(rows):
                dst[SMALL * i + 2 * q + comp : SMALL * i + 2 * q + comp + 1, :] = moved[
                    row0 + i : row0 + i + 1, :
                ]


def row_conv(w_ref, src, src0, lo, hi, ch, emit):
    spare = w_ref.shape[1] // 3 - (BLOCK + 2) * ch
    row = lo
    while row < hi:
        start = min(row, hi - BLOCK)
        skip = row - start
        first = (start - 1 - src0) * ch
        parts = []
        for q in range(3):
            parts.append(src[q, first : first + (BLOCK + 2) * ch, :])
            if spare:
                parts.append(jnp.zeros((spare, src.shape[2]), BF16))
        y = jnp.dot(
            w_ref[skip * ch : BLOCK * ch, :],
            jnp.concatenate(parts, axis=0),
            preferred_element_type=F32,
        )
        for k in range(BLOCK - skip):
            emit(row + k, y[k * ch : (k + 1) * ch])
        row = start + BLOCK


def chain(x4, pre, m_a, m_b, even, w4, w3, w2, d3, d2, d1, rows, ch):
    e3, e2, e1 = BORDERS

    def mask_rows(layer, row):
        if rows <= row < 2 * rows:
            return pre[layer, row - rows]
        above = row < rows
        border, start = ((e1, e3 + e2), (e2, e3), (e3, 0))[layer]
        k = start + (row - (rows - border) if above else row - 2 * rows)
        a, b = (m[k * ch : (k + 1) * ch, :] for m in (m_a, m_b))
        return jnp.where(even, b, a) if above else jnp.where(even, a, b)

    def store(dst, layer, first):
        def emit(row, e):
            d = e.astype(BF16)
            d = jnp.where(mask_rows(layer, row) > 0, d, jnp.zeros_like(d))
            at = slice((row - first) * ch, (row - first + 1) * ch)
            if len(dst.shape) == 2:
                dst[at, :] = d
            else:
                for q in range(3):
                    dst[q, at, :] = lane_roll(d, q - 1) if q != 1 else d

        return emit

    row, emit = rows - e3, store(d3, 2, rows - e3)
    while row < 2 * rows + e3:
        count = min(BLOCK4, 2 * rows + e3 - row)
        rhs = x4[SMALL * (row - 1) : SMALL * (row + count + 1), :].astype(BF16)
        y = jnp.dot(
            w4[: count * ch, : SMALL * (count + 2)], rhs, preferred_element_type=F32
        )
        for k in range(count):
            emit(row + k, y[k * ch : (k + 1) * ch])
        row += count
    row_conv(w3, d3, rows - e3, rows - e2, 2 * rows + e2, ch, store(d2, 1, rows - e2))
    empty = jnp.zeros((EMPTY * ch, d1.shape[-1]), BF16)
    d1[: EMPTY * ch, :] = empty
    d1[(rows + EMPTY) * ch :, :] = empty
    row_conv(w2, d2, rows - e2, rows, 2 * rows, ch, store(d1, 0, rows - EMPTY))


def first_conv(w1, d1, src0, lo, hi, ch, emit):
    row = lo
    while row < hi:
        start = min(row, hi - BLOCK)
        rhs = d1[(start - 1 - src0) * ch : (start + BLOCK + 1 - src0) * ch, :]
        y = jnp.dot(w1[...], rhs, preferred_element_type=F32)
        e = (
            y[SMALL : 2 * SMALL]
            + lane_roll(y[:SMALL], -1)
            + lane_roll(y[2 * SMALL : 3 * SMALL], 1)
        )
        for k in range(row - start, BLOCK):
            emit(start + k, [e[2 * k + comp : 2 * k + comp + 1, :] for comp in range(2)])
        row = start + BLOCK


def weight_terms(x4, d3, d2, d1, pre, x0s, rows, ch):
    dims = (((1,), (1,)), ((), ()))

    def product(a, b):
        return lax.dot_general(a, b, dims, preferred_element_type=F32)

    def three(ref, row, border):
        row -= rows - border
        return ref[1, (row - 1) * ch : (row + 2) * ch, :]

    def lanes(values):
        return jnp.concatenate(list(values), axis=1)

    def source(layer, i):
        a = pre[layer, i]
        return jnp.maximum(a, jnp.zeros_like(a))

    def moved(layer, i):
        h = source(layer, i)
        return jnp.concatenate([lane_roll(h, 1), h, lane_roll(h, -1)], axis=0)

    each = range(rows)
    return (
        product(
            lanes(x0s[SMALL * i : SMALL * (i + 3), :].astype(BF16) for i in each),
            lanes(d1[(i + EMPTY) * ch : (i + EMPTY + 1) * ch, :] for i in each),
        ),
        product(
            lanes(three(d2, rows + i, BORDERS[1]) for i in each),
            lanes(moved(0, i) for i in each),
        ),
        product(
            lanes(three(d3, rows + i, BORDERS[0]) for i in each),
            lanes(moved(1, i) for i in each),
        ),
        product(
            lanes(
                x4[SMALL * (rows + i - 1) : SMALL * (rows + i + 2), :].astype(BF16)
                for i in each
            ),
            lanes(source(2, i) for i in each),
        ),
    )


def pack_rows(ch):
    n = 3 * ch
    return -(-(2 * n + n // 2 + 3 * SMALL) // 32) * 32


def pack_terms(t_ref, terms, ch, before=None):
    g1, g2, g3, g4 = terms
    n = 3 * ch
    low = 2 * n + n // 2
    tail = jnp.concatenate([g2[:, LANES:], g3[:, LANES:]], axis=1)
    wide = tail.shape[1]
    parts = (
        (0, n, 0, LANES, g2[:, :LANES]),
        (n, 2 * n, 0, LANES, g3[:, :LANES]),
        (2 * n, low, 0, wide, tail[: n // 2]),
        (2 * n, low, wide, 2 * wide, tail[n // 2 :]),
        (low, low + 3 * SMALL, 0, 2 * ch, jnp.concatenate([g4, g1], axis=1)),
    )
    t_ref[2 * n :, :] = jnp.zeros((t_ref.shape[0] - 2 * n, LANES), F32)
    for r0, r1, c0, c1, value in parts:
        if before is not None:
            value = value + before[r0:r1, c0:c1]
        t_ref[r0:r1, c0:c1] = value


def gather_kernel(
    axis, takes, rows, ch, base, step, with_d4,
    pre_hbm, states, cot, out_a, out_b, sems, u, g,
):
    even = lax.rem(lax.axis_index(axis), 2) == 0
    copies = [pltpu.make_async_copy(states.at[step], u, sems.at[0])]
    if with_d4:
        copies.append(pltpu.make_async_copy(cot, g, sems.at[1]))
    first = len(copies)
    for layer, count, dst in takes:
        low, high = 0, (rows - count) * ch
        for out, start in (
            (out_a, jnp.where(even, high, low)),
            (out_b, jnp.where(even, low, high)),
        ):
            copies.append(
                pltpu.make_async_copy(
                    pre_hbm.at[step, layer, pl.ds(pl.multiple_of(start, ch), count * ch)],
                    out.at[pl.ds(dst * ch, count * ch)],
                    sems.at[len(copies)],
                )
            )
    for copy in copies:
        copy.start()
    for copy in copies[:first]:
        copy.wait()
    planes = [split_terms(u[comp]) for comp in range(2)]
    if with_d4:
        planes.append(jnp.concatenate([g[0], g[1]], axis=0).astype(BF16))
    for i, plane in enumerate(planes):
        for out in (out_a, out_b):
            out[base + 2 * rows * i : base + 2 * rows * (i + 1), :] = plane
    for copy in copies[first:]:
        copy.wait()


def weights_kernel(ch, w1, w2, w3, w4, o1, o2, o3, o4):
    for w, o in ((w3, o3), (w2, o2)):
        wide = o.shape[1] // 3
        for q in range(3):
            block = jnp.concatenate([w[3 * (2 - m) + q].astype(F32) for m in range(3)], axis=0)
            block = block.T.astype(BF16)
            for b in range(BLOCK):
                o[b * ch : (b + 1) * ch, q * wide : (q + 1) * wide] = placed(block, b * ch, wide)
    zero = jnp.zeros((SMALL - 6, ch), F32)
    block = jnp.concatenate(
        [
            piece
            for m in range(3)
            for piece in [w4[3 * (2 - m) + q].astype(F32) for q in range(3)] + [zero]
        ],
        axis=0,
    )
    block = block.T.astype(BF16)
    for b in range(BLOCK4):
        o4[b * ch : (b + 1) * ch, :] = placed(block, b * SMALL, o4.shape[1])
    rows = []
    for q in range(3):
        block = jnp.concatenate([w1[3 * (2 - m) + q].astype(F32) for m in range(3)], axis=1)
        for b in range(BLOCK):
            rows.append(placed(block, b * ch, o1.shape[1]))
        rows.append(jnp.zeros((SMALL - 2 * BLOCK, o1.shape[1]), F32))
    o1[...] = jnp.concatenate(rows, axis=0).astype(BF16)


def placed(block, column, width):
    parts = [block]
    if column:
        parts.insert(0, jnp.zeros((block.shape[0], column), block.dtype))
    rest = width - column - block.shape[1]
    if rest:
        parts.append(jnp.zeros((block.shape[0], rest), block.dtype))
    return jnp.concatenate(parts, axis=1)


def partial_input(w1, d1, own, out, rows, ch):
    out[2 * rows :, :] = jnp.zeros((SMALL, out.shape[1]), F32)

    def emit(row, values):
        i = row - rows
        for comp in range(2):
            if 0 <= i < rows:
                k = rows * comp + i
                out[k : k + 1, :] = own(comp, i) + values[comp]
            else:
                k = 2 * rows + 2 * comp + (i > 0)
                out[k : k + 1, :] = values[comp]

    first_conv(w1, d1, rows - EMPTY, rows - 1, 2 * rows + 1, ch, emit)


def whole_input(gh, gh_a, gh_b, lam, rows, even):
    a, b = gh_a[...], gh_b[...]
    above, below = jnp.where(even, b, a), jnp.where(even, a, b)
    for comp in range(2):
        own = slice(rows * comp, rows * (comp + 1))
        lam[comp, :rows, :] = above[own]
        lam[comp, rows : 2 * rows, :] = gh[own, :]
        lam[comp, 2 * rows :, :] = below[own]
        k = 2 * rows + 2 * comp
        for row, part in (
            (rows - 1, gh[k : k + 1, :]),
            (rows, above[k + 1 : k + 2]),
            (2 * rows - 1, below[k : k + 1]),
            (2 * rows, gh[k + 1 : k + 2, :]),
        ):
            lam[comp, row : row + 1, :] += part


def border_states(states, step, m_a, m_b, rows, ch, even):
    a = border_planes(m_a, sum(BORDERS) * ch, rows, 2)
    b = border_planes(m_b, sum(BORDERS) * ch, rows, 2)
    return [joined(a[comp], states[step, comp], b[comp], even) for comp in range(2)]


def back_kernel(axis, rows, ch, cot, pre, m_a, m_b, w4, w3, w2, w1, gh, x4, d3, d2, d1):
    even = lax.rem(lax.axis_index(axis), 2) == 0
    base = sum(BORDERS) * ch + 4 * rows
    a, b = (m[base : base + 2 * rows, :].astype(F32) for m in (m_a, m_b))
    planes = [
        joined(
            a[rows * comp : rows * (comp + 1)], cot[comp], b[rows * comp : rows * (comp + 1)], even
        )
        for comp in range(2)
    ]
    fill_small(x4, planes, 3 * rows, 0, 1)
    chain(x4, pre.at[0], m_a, m_b, even, w4, w3, w2, d3, d2, d1, rows, ch)
    partial_input(w1, d1, lambda comp, i: cot[comp, i : i + 1, :], gh, rows, ch)


def term_kernel(axis, rows, ch, x4, d3, d2, d1, pre, states, m_a, m_b, t_out, u_out, x0s):
    even = lax.rem(lax.axis_index(axis), 2) == 0
    u = border_states(states, 1, m_a, m_b, rows, ch, even)
    for comp in range(2):
        u_out[comp] = u[comp]
    fill_small(x0s, half_step(*u), rows + 2, rows - 1, -1)
    pack_terms(t_out, weight_terms(x4, d3, d2, d1, pre.at[0], x0s, rows, ch), ch)


def front_kernel(
    axis, rows, ch,
    gh, gh_a, gh_b, u1, states, pre, m_a, m_b, w4, w3, w2, before,
    keep, give, g_out, u_out, d1, x4, d3, d2, x0s, total, lam,
):
    even = lax.rem(lax.axis_index(axis), 2) == 0
    whole_input(gh, gh_a, gh_b, lam, rows, even)
    planes = half_step_transpose(u1[0], u1[1], lam[0], lam[1])
    for comp in range(2):
        g_out[comp] = planes[comp][rows : 2 * rows]
    fill_small(x4, planes, 3 * rows, 0, 1)
    u = border_states(states, 0, m_a, m_b, rows, ch, even)
    for comp in range(2):
        u_out[comp] = u[comp]
    fill_small(x0s, half_step(*u), rows + 2, rows - 1, -1)
    chain(x4, pre.at[0], m_a, m_b, even, w4, w3, w2, d3, d2, d1, rows, ch)
    pack_terms(total, weight_terms(x4, d3, d2, d1, pre.at[0], x0s, rows, ch), ch, before)
    half = total.shape[0] // 2
    a, b = total[:half, :], total[half:, :]
    keep[...] = jnp.where(even, a, b)
    give[...] = jnp.where(even, b, a)


def input_kernel(rows, ch, g, d1, w1, gh):
    partial_input(w1, d1, lambda comp, i: g[comp, i : i + 1, :], gh, rows, ch)


def last_kernel(axis, rows, gh, gh_a, gh_b, u, out, lam):
    even = lax.rem(lax.axis_index(axis), 2) == 0
    whole_input(gh, gh_a, gh_b, lam, rows, even)
    planes = half_step_transpose(u[0], u[1], lam[0], lam[1])
    for comp in range(2):
        out[comp] = planes[comp][rows : 2 * rows]


def unpack_kernel(axis, ch, factor, mine, other, o1, o2, o3, o4):
    even = lax.rem(lax.axis_index(axis), 2) == 0
    a, b = mine[...].astype(F32), other[...].astype(F32)
    t = factor * jnp.concatenate([jnp.where(even, a, b), jnp.where(even, b, a)], axis=0)
    n = 3 * ch
    rest = n - LANES
    wide = 2 * rest
    low = 2 * n + n // 2
    tail = t[2 * n : low]
    tail = jnp.concatenate([tail[:, :wide], tail[:, wide : 2 * wide]], axis=0)
    g2 = jnp.concatenate([t[:n], tail[:, :rest]], axis=1)
    g3 = jnp.concatenate([t[n : 2 * n], tail[:, rest:]], axis=1)
    g4 = t[low : low + 3 * SMALL, :ch]
    g1 = t[low : low + 3 * SMALL, ch : 2 * ch]
    for m in range(3):
        for q in range(3):
            tap = 3 * (2 - m) + q
            o2[tap] = g2[m * ch : (m + 1) * ch, q * ch : (q + 1) * ch]
            o3[tap] = g3[m * ch : (m + 1) * ch, q * ch : (q + 1) * ch]
            small = slice(m * SMALL + 2 * q, m * SMALL + 2 * q + 2)
            o4[tap] = g4[small]
            o1[3 * m + q] = g1[small]


VMEM = pl.BlockSpec(memory_space=pltpu.VMEM)


def call(kernel, outs, scratch, args, specs=None, limit=24 << 20, flops=10**8):
    specs = specs or {}
    return pl.pallas_call(
        kernel,
        out_shape=outs,
        grid=(1,) if specs else (),
        in_specs=[specs.get(i, VMEM) for i in range(len(args))],
        out_specs=jax.tree.map(lambda _: VMEM, outs),
        scratch_shapes=scratch,
        compiler_params=pltpu.CompilerParams(vmem_limit_bytes=limit),
        cost_estimate=pl.CostEstimate(
            flops=flops, bytes_accessed=2 * 10**6, transcendentals=0
        ),
    )(*args)


def on_device(states, pre_acts, cotangent, weight_in, weight_second, weight_third, weight_out):
    axis = "gx"
    count = lax.axis_size(axis)
    _, _, rows, width = states.shape
    ch = pre_acts.shape[3]
    flat = pre_acts.reshape(pre_acts.shape[:2] + (rows * ch, width))

    pair_a = [(i, i ^ 1) for i in range(count)]
    pair_b = [(i, (i + 1) % count if i % 2 else (i - 1) % count) for i in range(count)]

    def swap(for_a, for_b):
        b = lax.ppermute(for_b, axis, pair_b)
        a = lax.ppermute(for_a, axis, pair_a)
        return a, b

    def shape(*dims, dtype=F32):
        return jax.ShapeDtypeStruct(dims, dtype)

    def borders(step, with_d4, room):
        takes, total = [], 0
        for layer, border in zip((2, 1, 0), BORDERS):
            if not border:
                continue
            takes.append((layer, border, total))
            total += border
        base = total * ch
        out = shape(base + (6 if with_d4 else 4) * rows, width, dtype=BF16)
        pack = pl.pallas_call(
            functools.partial(gather_kernel, axis, takes, rows, ch, base, step, with_d4),
            out_shape=[out, out],
            in_specs=[pl.BlockSpec(memory_space=pltpu.HBM)] * 3,
            out_specs=[VMEM, VMEM],
            scratch_shapes=[pltpu.SemaphoreType.DMA((2 * len(takes) + 2,))]
            + [pltpu.VMEM((2, rows, width), F32)] * 2,
            compiler_params=pltpu.CompilerParams(vmem_limit_bytes=VMEM_BYTES - room),
        )
        a, b = pack(flat, states, cotangent)
        return swap(a, b)

    m1_a, m1_b = borders(1, True, 3 << 20)
    m0_a, m0_b = borders(0, False, 56 << 20)

    def bands(n, m):
        return shape(n, m, dtype=BF16)

    wide = -(-(BLOCK + 2) * ch // LANES) * LANES
    w1, w2, w3, w4 = call(
        functools.partial(weights_kernel, ch),
        [
            bands(3 * SMALL, (BLOCK + 2) * ch),
            bands(BLOCK * ch, 3 * wide),
            bands(BLOCK * ch, 3 * wide),
            bands(BLOCK4 * ch, (BLOCK4 + 2) * SMALL),
        ],
        [],
        (jnp.swapaxes(weight_in, 1, 2), weight_second, weight_third, weight_out),
    )

    def pre_spec(step):
        return pl.BlockSpec((1,) + pre_acts.shape[1:], lambda *_: (step, 0, 0, 0, 0))

    def d_shape(border):
        return shape((rows + 2 * border) * ch, width, dtype=BF16)

    def scratch(*shapes):
        return [pltpu.VMEM(s.shape, s.dtype) for s in shapes]

    x4_shape = shape(3 * rows * SMALL, width)
    x0_shape = shape((rows + 2) * SMALL, width)
    d_shapes = [
        shape(3, *d_shape(BORDERS[0]).shape, dtype=BF16),
        shape(3, *d_shape(BORDERS[1]).shape, dtype=BF16),
        d_shape(EMPTY),
    ]
    planes = shape(2, 3 * rows, width)
    part = shape(2 * rows + SMALL, width)
    total = shape(pack_rows(ch), LANES)
    half = shape(pack_rows(ch) // 2, LANES)
    gh, x4, d3, d2, d1 = call(
        functools.partial(back_kernel, axis, rows, ch),
        [part, x4_shape] + d_shapes,
        [],
        (cotangent, pre_acts, m1_a, m1_b, w4, w3, w2, w1),
        {1: pre_spec(1)},
    )
    gh_a, gh_b = swap(gh, gh)
    before, u1 = call(
        functools.partial(term_kernel, axis, rows, ch),
        [total, planes],
        scratch(x0_shape),
        (x4, d3, d2, d1, pre_acts, states, m1_a, m1_b),
        {4: pre_spec(1)},
    )
    keep, give, g, u0, d1 = call(
        functools.partial(front_kernel, axis, rows, ch),
        [half, half, shape(2, rows, width), planes, d_shapes[2]],
        scratch(x4_shape, d_shapes[0], d_shapes[1], x0_shape, total, planes),
        (gh, gh_a, gh_b, u1, states, pre_acts, m0_a, m0_b, w4, w3, w2, before),
        {5: pre_spec(0)},
    )
    gh0 = call(functools.partial(input_kernel, rows, ch), part, [], (g, d1, w1))
    gh0_a, gh0_b = swap(gh0, gh0)
    adjoint = call(
        functools.partial(last_kernel, axis, rows),
        shape(2, rows, width),
        scratch(planes),
        (gh0, gh0_a, gh0_b, u0),
    )

    mine = keep + lax.ppermute(give, axis, pair_a)
    bit = 2
    while bit < count:
        mine = mine.astype(BF16)
        got = lax.ppermute(mine, axis, [(i, i ^ bit) for i in range(count)])
        if 2 * bit >= count:
            got, adjoint = lax.optimization_barrier((got, adjoint))
        mine = mine.astype(F32) + got.astype(F32)
        bit *= 2
    other = lax.ppermute(mine, axis, pair_a)
    factor = 1.0 / math.sqrt(rows * count * width)
    g1, g2, g3, g4 = call(
        functools.partial(unpack_kernel, axis, ch, factor),
        [
            shape(*w)
            for w in (
                weight_out.shape[:1] + (weight_in.shape[2], ch),
                weight_second.shape,
                weight_third.shape,
                weight_out.shape,
            )
        ],
        [],
        (mine, other),
    )
    return adjoint, jnp.swapaxes(g1, 1, 2), g2, g3, g4


def solution(mesh):
    return jax.shard_map(
        on_device,
        mesh=mesh,
        in_specs=(
            P(None, "groups", "gx", None),
            P(None, None, ("groups", "gx"), None, None),
            P("groups", "gx", None),
            P(),
            P(),
            P(),
            P(),
        ),
        out_specs=(
            P("groups", "gx", None),
            P("groups", None, None),
            P("groups", None, None),
            P("groups", None, None),
            P("groups", None, None),
        ),
        check_vma=False,
    )
```

```python
import functools
import math

import jax
import jax.numpy as jnp
from jax import lax
from jax.experimental import pallas as pl
from jax.experimental.pallas import tpu as pltpu
from jax.sharding import PartitionSpec as P


STEP = 0.25
VISC = 0.4
LANES = 128
BLOCK = 3
BLOCK4 = 4
VMEM_BYTES = 67043328
BORDERS = (2, 1, 0)
EMPTY = 2
SMALL = 8

F32 = jnp.float32
BF16 = jnp.bfloat16


def lane_roll(x, shift):
    width = x.shape[-1]
    return pltpu.roll(x, shift % width, x.ndim - 1)


def row_roll(x, shift):
    return pltpu.roll(x, shift % x.shape[0], 0)


def half_step(r, c):
    face = 0.25 * (r + row_roll(r, -1))
    side = 0.25 * (c + lane_roll(c, -1))
    outs = []
    for f in (r, c):
        down, right = row_roll(f, -1), lane_roll(f, -1)
        p = face * (f + down)
        q = side * (f + right)
        div = p - row_roll(p, 1) + (q - lane_roll(q, 1))
        lap = down + row_roll(f, 1) + right + lane_roll(f, 1) - 4.0 * f
        outs.append(f + STEP * (VISC * lap - div))
    return outs


def half_step_transpose(r, c, lr, lc):
    face = 0.25 * (r + row_roll(r, -1))
    side = 0.25 * (c + lane_roll(c, -1))
    outs = []
    extra_r = None
    extra_c = None
    for f, l in ((r, lr), (c, lc)):
        l_down, l_right = row_roll(l, -1), lane_roll(l, -1)
        a = STEP * (l_down - l)
        b = STEP * (l_right - l)
        ap, bq = a * face, b * side
        lap = l_down + row_roll(l, 1) + l_right + lane_roll(l, 1) - 4.0 * l
        outs.append(
            l + (STEP * VISC) * lap + (ap + row_roll(ap, 1)) + (bq + lane_roll(bq, 1))
        )
        af = a * (0.25 * (f + row_roll(f, -1)))
        bf = b * (0.25 * (f + lane_roll(f, -1)))
        extra_r = af if extra_r is None else extra_r + af
        extra_c = bf if extra_c is None else extra_c + bf
    return [
        outs[0] + (extra_r + row_roll(extra_r, 1)),
        outs[1] + (extra_c + lane_roll(extra_c, 1)),
    ]


def joined(a, own, b, even):
    return jnp.concatenate([jnp.where(even, b, a), own, jnp.where(even, a, b)], axis=0)


def split_terms(x):
    high = x.astype(BF16).astype(F32)
    return jnp.concatenate([high, x - high], axis=0).astype(BF16)


def border_planes(ref, first, rows, count):
    parts = [
        ref[first + 2 * rows * i : first + 2 * rows * (i + 1), :].astype(F32)
        for i in range(count)
    ]
    return [p[:rows] + p[rows:] for p in parts]


def fill_small(dst, planes, rows, row0, sign):
    dst[...] = jnp.zeros(dst.shape, F32)
    for comp, plane in enumerate(planes):
        value = plane.astype(BF16).astype(F32)
        for q in range(3):
            moved = value if q == 1 else lane_roll(value, sign * (q - 1))
            for i in range(rows):
                dst[SMALL * i + 2 * q + comp : SMALL * i + 2 * q + comp + 1, :] = moved[
                    row0 + i : row0 + i + 1, :
                ]


def row_conv(w_ref, src, src0, lo, hi, ch, emit):
    spare = w_ref.shape[1] // 3 - (BLOCK + 2) * ch
    row = lo
    while row < hi:
        start = min(row, hi - BLOCK)
        skip = row - start
        first = (start - 1 - src0) * ch
        parts = []
        for q in range(3):
            parts.append(src[q, first : first + (BLOCK + 2) * ch, :])
            if spare:
                parts.append(jnp.zeros((spare, src.shape[2]), BF16))
        y = jnp.dot(
            w_ref[skip * ch : BLOCK * ch, :],
            jnp.concatenate(parts, axis=0),
            preferred_element_type=F32,
        )
        for k in range(BLOCK - skip):
            emit(row + k, y[k * ch : (k + 1) * ch])
        row = start + BLOCK


def chain(x4, pre, m_a, m_b, even, w4, w3, w2, d3, d2, d1, rows, ch):
    e3, e2, e1 = BORDERS

    def mask_rows(layer, row):
        if rows <= row < 2 * rows:
            return pre[layer, row - rows]
        above = row < rows
        border, start = ((e1, e3 + e2), (e2, e3), (e3, 0))[layer]
        k = start + (row - (rows - border) if above else row - 2 * rows)
        a, b = (m[k * ch : (k + 1) * ch, :] for m in (m_a, m_b))
        return jnp.where(even, b, a) if above else jnp.where(even, a, b)

    def store(dst, layer, first):
        def emit(row, e):
            d = e.astype(BF16)
            d = jnp.where(mask_rows(layer, row) > 0, d, jnp.zeros_like(d))
            at = slice((row - first) * ch, (row - first + 1) * ch)
            if len(dst.shape) == 2:
                dst[at, :] = d
            else:
                for q in range(3):
                    dst[q, at, :] = lane_roll(d, q - 1) if q != 1 else d

        return emit

    row, emit = rows - e3, store(d3, 2, rows - e3)
    while row < 2 * rows + e3:
        count = min(BLOCK4, 2 * rows + e3 - row)
        rhs = x4[SMALL * (row - 1) : SMALL * (row + count + 1), :].astype(BF16)
        y = jnp.dot(
            w4[: count * ch, : SMALL * (count + 2)], rhs, preferred_element_type=F32
        )
        for k in range(count):
            emit(row + k, y[k * ch : (k + 1) * ch])
        row += count
    row_conv(w3, d3, rows - e3, rows - e2, 2 * rows + e2, ch, store(d2, 1, rows - e2))
    empty = jnp.zeros((EMPTY * ch, d1.shape[-1]), BF16)
    d1[: EMPTY * ch, :] = empty
    d1[(rows + EMPTY) * ch :, :] = empty
    row_conv(w2, d2, rows - e2, rows, 2 * rows, ch, store(d1, 0, rows - EMPTY))


def first_conv(w1, d1, src0, lo, hi, ch, emit):
    row = lo
    while row < hi:
        start = min(row, hi - BLOCK)
        rhs = d1[(start - 1 - src0) * ch : (start + BLOCK + 1 - src0) * ch, :]
        y = jnp.dot(w1[...], rhs, preferred_element_type=F32)
        e = (
            y[SMALL : 2 * SMALL]
            + lane_roll(y[:SMALL], -1)
            + lane_roll(y[2 * SMALL : 3 * SMALL], 1)
        )
        for k in range(row - start, BLOCK):
            emit(start + k, [e[2 * k + comp : 2 * k + comp + 1, :] for comp in range(2)])
        row = start + BLOCK


def weight_terms(x4, d3, d2, d1, pre, x0s, rows, ch):
    dims = (((1,), (1,)), ((), ()))

    def product(a, b):
        return lax.dot_general(a, b, dims, preferred_element_type=F32)

    def three(ref, row, border):
        row -= rows - border
        return ref[1, (row - 1) * ch : (row + 2) * ch, :]

    def lanes(values):
        return jnp.concatenate(list(values), axis=1)

    def source(layer, i):
        a = pre[layer, i]
        return jnp.maximum(a, jnp.zeros_like(a))

    def moved(layer, i):
        h = source(layer, i)
        return jnp.concatenate([lane_roll(h, 1), h, lane_roll(h, -1)], axis=0)

    each = range(rows)
    return (
        product(
            lanes(x0s[SMALL * i : SMALL * (i + 3), :].astype(BF16) for i in each),
            lanes(d1[(i + EMPTY) * ch : (i + EMPTY + 1) * ch, :] for i in each),
        ),
        product(
            lanes(three(d2, rows + i, BORDERS[1]) for i in each),
            lanes(moved(0, i) for i in each),
        ),
        product(
            lanes(three(d3, rows + i, BORDERS[0]) for i in each),
            lanes(moved(1, i) for i in each),
        ),
        product(
            lanes(
                x4[SMALL * (rows + i - 1) : SMALL * (rows + i + 2), :].astype(BF16)
                for i in each
            ),
            lanes(source(2, i) for i in each),
        ),
    )


def pack_rows(ch):
    n = 3 * ch
    return -(-(2 * n + n // 2 + 3 * SMALL) // 32) * 32


def pack_terms(t_ref, terms, ch, before=None):
    g1, g2, g3, g4 = terms
    n = 3 * ch
    low = 2 * n + n // 2
    tail = jnp.concatenate([g2[:, LANES:], g3[:, LANES:]], axis=1)
    wide = tail.shape[1]
    parts = (
        (0, n, 0, LANES, g2[:, :LANES]),
        (n, 2 * n, 0, LANES, g3[:, :LANES]),
        (2 * n, low, 0, wide, tail[: n // 2]),
        (2 * n, low, wide, 2 * wide, tail[n // 2 :]),
        (low, low + 3 * SMALL, 0, 2 * ch, jnp.concatenate([g4, g1], axis=1)),
    )
    t_ref[2 * n :, :] = jnp.zeros((t_ref.shape[0] - 2 * n, LANES), F32)
    for r0, r1, c0, c1, value in parts:
        if before is not None:
            value = value + before[r0:r1, c0:c1]
        t_ref[r0:r1, c0:c1] = value


def gather_kernel(axis, takes, rows, ch, base, step, late, pre_hbm, more, out_a, out_b, sems, buf):
    even = lax.rem(lax.axis_index(axis), 2) == 0
    copies = [pltpu.make_async_copy(more, buf, sems.at[0])]
    for layer, count, dst in takes:
        low, high = 0, (rows - count) * ch
        for out, start in (
            (out_a, jnp.where(even, high, low)),
            (out_b, jnp.where(even, low, high)),
        ):
            copies.append(
                pltpu.make_async_copy(
                    pre_hbm.at[step, layer, pl.ds(pl.multiple_of(start, ch), count * ch)],
                    out.at[pl.ds(dst * ch, count * ch)],
                    sems.at[len(copies)],
                )
            )
    for copy in copies:
        copy.start()
    copies[0].wait()
    if late:
        planes = [split_terms(buf[k, comp]) for k in range(2) for comp in range(2)]
    else:
        planes = [jnp.concatenate([buf[0], buf[1]], axis=0).astype(BF16)]
    for i, plane in enumerate(planes):
        for out in (out_a, out_b):
            out[base + 2 * rows * i : base + 2 * rows * (i + 1), :] = plane
    for copy in copies[1:]:
        copy.wait()


def weights_kernel(ch, w1, w2, w3, w4, o1, o2, o3, o4):
    for w, o in ((w3, o3), (w2, o2)):
        wide = o.shape[1] // 3
        for q in range(3):
            block = jnp.concatenate([w[3 * (2 - m) + q].astype(F32) for m in range(3)], axis=0)
            block = block.T.astype(BF16)
            for b in range(BLOCK):
                o[b * ch : (b + 1) * ch, q * wide : (q + 1) * wide] = placed(block, b * ch, wide)
    zero = jnp.zeros((SMALL - 6, ch), F32)
    block = jnp.concatenate(
        [
            piece
            for m in range(3)
            for piece in [w4[3 * (2 - m) + q].astype(F32) for q in range(3)] + [zero]
        ],
        axis=0,
    )
    block = block.T.astype(BF16)
    for b in range(BLOCK4):
        o4[b * ch : (b + 1) * ch, :] = placed(block, b * SMALL, o4.shape[1])
    rows = []
    for q in range(3):
        block = jnp.concatenate([w1[3 * (2 - m) + q].astype(F32) for m in range(3)], axis=1)
        for b in range(BLOCK):
            rows.append(placed(block, b * ch, o1.shape[1]))
        rows.append(jnp.zeros((SMALL - 2 * BLOCK, o1.shape[1]), F32))
    o1[...] = jnp.concatenate(rows, axis=0).astype(BF16)


def placed(block, column, width):
    parts = [block]
    if column:
        parts.insert(0, jnp.zeros((block.shape[0], column), block.dtype))
    rest = width - column - block.shape[1]
    if rest:
        parts.append(jnp.zeros((block.shape[0], rest), block.dtype))
    return jnp.concatenate(parts, axis=1)


def partial_input(w1, d1, own, out, rows, ch):
    out[2 * rows :, :] = jnp.zeros((SMALL, out.shape[1]), F32)

    def emit(row, values):
        i = row - rows
        for comp in range(2):
            if 0 <= i < rows:
                k = rows * comp + i
                out[k : k + 1, :] = own(comp, i) + values[comp]
            else:
                k = 2 * rows + 2 * comp + (i > 0)
                out[k : k + 1, :] = values[comp]

    first_conv(w1, d1, rows - EMPTY, rows - 1, 2 * rows + 1, ch, emit)


def whole_input(gh, gh_a, gh_b, lam, rows, even):
    a, b = gh_a[...], gh_b[...]
    above, below = jnp.where(even, b, a), jnp.where(even, a, b)
    for comp in range(2):
        own = slice(rows * comp, rows * (comp + 1))
        lam[comp, :rows, :] = above[own]
        lam[comp, rows : 2 * rows, :] = gh[own, :]
        lam[comp, 2 * rows :, :] = below[own]
        k = 2 * rows + 2 * comp
        for row, part in (
            (rows - 1, gh[k : k + 1, :]),
            (rows, above[k + 1 : k + 2]),
            (2 * rows - 1, below[k : k + 1]),
            (2 * rows, gh[k + 1 : k + 2, :]),
        ):
            lam[comp, row : row + 1, :] += part


def border_states(states, step, m_a, m_b, rows, ch, even):
    first = sum(BORDERS) * ch + 4 * rows * step
    a = border_planes(m_a, first, rows, 2)
    b = border_planes(m_b, first, rows, 2)
    return [joined(a[comp], states[step, comp], b[comp], even) for comp in range(2)]


def back_kernel(axis, rows, ch, cot, pre, m_a, m_b, w4, w3, w2, w1, gh, x4, d3, d2, d1):
    even = lax.rem(lax.axis_index(axis), 2) == 0
    base = sum(BORDERS) * ch
    a, b = (m[base : base + 2 * rows, :].astype(F32) for m in (m_a, m_b))
    planes = [
        joined(
            a[rows * comp : rows * (comp + 1)], cot[comp], b[rows * comp : rows * (comp + 1)], even
        )
        for comp in range(2)
    ]
    fill_small(x4, planes, 3 * rows, 0, 1)
    chain(x4, pre.at[0], m_a, m_b, even, w4, w3, w2, d3, d2, d1, rows, ch)
    partial_input(w1, d1, lambda comp, i: cot[comp, i : i + 1, :], gh, rows, ch)


def term_kernel(
    axis, rows, ch,
    x4, d3, d2, d1, pre, states, m_a, m_b,
    t_out, u1, u0, x0s, x1s,
):
    even = lax.rem(lax.axis_index(axis), 2) == 0
    for step, out, small in ((1, u1, x1s), (0, u0, x0s)):
        u = border_states(states, step, m_a, m_b, rows, ch, even)
        for comp in range(2):
            out[comp] = u[comp]
        fill_small(small, half_step(*u), rows + 2, rows - 1, -1)
    pack_terms(t_out, weight_terms(x4, d3, d2, d1, pre.at[0], x1s, rows, ch), ch)


def front_kernel(
    axis, rows, ch,
    gh, gh_a, gh_b, u1, x0s, pre, m_a, m_b, w4, w3, w2, before,
    keep, give, g_out, d1, x4, d3, d2, total, lam,
):
    even = lax.rem(lax.axis_index(axis), 2) == 0
    whole_input(gh, gh_a, gh_b, lam, rows, even)
    planes = half_step_transpose(u1[0], u1[1], lam[0], lam[1])
    for comp in range(2):
        g_out[comp] = planes[comp][rows : 2 * rows]
    fill_small(x4, planes, 3 * rows, 0, 1)
    chain(x4, pre.at[0], m_a, m_b, even, w4, w3, w2, d3, d2, d1, rows, ch)
    pack_terms(total, weight_terms(x4, d3, d2, d1, pre.at[0], x0s, rows, ch), ch, before)
    half = total.shape[0] // 2
    a, b = total[:half, :], total[half:, :]
    keep[...] = jnp.where(even, a, b)
    give[...] = jnp.where(even, b, a)


def input_kernel(rows, ch, g, d1, w1, gh):
    partial_input(w1, d1, lambda comp, i: g[comp, i : i + 1, :], gh, rows, ch)


def last_kernel(axis, rows, gh, gh_a, gh_b, u, out, lam):
    even = lax.rem(lax.axis_index(axis), 2) == 0
    whole_input(gh, gh_a, gh_b, lam, rows, even)
    planes = half_step_transpose(u[0], u[1], lam[0], lam[1])
    for comp in range(2):
        out[comp] = planes[comp][rows : 2 * rows]


def unpack_kernel(axis, ch, factor, mine, other, o1, o2, o3, o4):
    even = lax.rem(lax.axis_index(axis), 2) == 0
    a, b = mine[...].astype(F32), other[...].astype(F32)
    t = factor * jnp.concatenate([jnp.where(even, a, b), jnp.where(even, b, a)], axis=0)
    n = 3 * ch
    rest = n - LANES
    wide = 2 * rest
    low = 2 * n + n // 2
    tail = t[2 * n : low]
    tail = jnp.concatenate([tail[:, :wide], tail[:, wide : 2 * wide]], axis=0)
    g2 = jnp.concatenate([t[:n], tail[:, :rest]], axis=1)
    g3 = jnp.concatenate([t[n : 2 * n], tail[:, rest:]], axis=1)
    g4 = t[low : low + 3 * SMALL, :ch]
    g1 = t[low : low + 3 * SMALL, ch : 2 * ch]
    for m in range(3):
        for q in range(3):
            tap = 3 * (2 - m) + q
            o2[tap] = g2[m * ch : (m + 1) * ch, q * ch : (q + 1) * ch]
            o3[tap] = g3[m * ch : (m + 1) * ch, q * ch : (q + 1) * ch]
            small = slice(m * SMALL + 2 * q, m * SMALL + 2 * q + 2)
            o4[tap] = g4[small]
            o1[3 * m + q] = g1[small]


VMEM = pl.BlockSpec(memory_space=pltpu.VMEM)


def call(kernel, outs, scratch, args, specs=None, limit=24 << 20, flops=10**8):
    specs = specs or {}
    return pl.pallas_call(
        kernel,
        out_shape=outs,
        grid=(1,) if specs else (),
        in_specs=[specs.get(i, VMEM) for i in range(len(args))],
        out_specs=jax.tree.map(lambda _: VMEM, outs),
        scratch_shapes=scratch,
        compiler_params=pltpu.CompilerParams(vmem_limit_bytes=limit),
        cost_estimate=pl.CostEstimate(
            flops=flops, bytes_accessed=2 * 10**6, transcendentals=0
        ),
    )(*args)


def on_device(states, pre_acts, cotangent, weight_in, weight_second, weight_third, weight_out):
    axis = "gx"
    count = lax.axis_size(axis)
    _, _, rows, width = states.shape
    ch = pre_acts.shape[3]
    flat = pre_acts.reshape(pre_acts.shape[:2] + (rows * ch, width))

    pair_a = [(i, i ^ 1) for i in range(count)]
    pair_b = [(i, (i + 1) % count if i % 2 else (i - 1) % count) for i in range(count)]

    def swap(for_a, for_b):
        b = lax.ppermute(for_b, axis, pair_b)
        a = lax.ppermute(for_a, axis, pair_a)
        return a, b

    def shape(*dims, dtype=F32):
        return jax.ShapeDtypeStruct(dims, dtype)

    def borders(step, late, room):
        takes, total = [], 0
        for layer, border in zip((2, 1, 0), BORDERS):
            if not border:
                continue
            takes.append((layer, border, total))
            total += border
        base = total * ch
        more = states if late else cotangent
        out = shape(base + 2 * rows * (4 if late else 1), width, dtype=BF16)
        pack = pl.pallas_call(
            functools.partial(gather_kernel, axis, takes, rows, ch, base, step, late),
            out_shape=[out, out],
            in_specs=[pl.BlockSpec(memory_space=pltpu.HBM)] * 2,
            out_specs=[VMEM, VMEM],
            scratch_shapes=[
                pltpu.SemaphoreType.DMA((2 * len(takes) + 1,)),
                pltpu.VMEM(more.shape, F32),
            ],
            compiler_params=pltpu.CompilerParams(vmem_limit_bytes=VMEM_BYTES - room),
        )
        a, b = pack(flat, more)
        return swap(a, b)

    m1_a, m1_b = borders(1, False, 3 << 20)
    m0_a, m0_b = borders(0, True, 56 << 20)

    def bands(n, m):
        return shape(n, m, dtype=BF16)

    wide = -(-(BLOCK + 2) * ch // LANES) * LANES
    w1, w2, w3, w4 = call(
        functools.partial(weights_kernel, ch),
        [
            bands(3 * SMALL, (BLOCK + 2) * ch),
            bands(BLOCK * ch, 3 * wide),
            bands(BLOCK * ch, 3 * wide),
            bands(BLOCK4 * ch, (BLOCK4 + 2) * SMALL),
        ],
        [],
        (jnp.swapaxes(weight_in, 1, 2), weight_second, weight_third, weight_out),
    )

    def pre_spec(step):
        return pl.BlockSpec((1,) + pre_acts.shape[1:], lambda *_: (step, 0, 0, 0, 0))

    def d_shape(border):
        return shape((rows + 2 * border) * ch, width, dtype=BF16)

    def scratch(*shapes):
        return [pltpu.VMEM(s.shape, s.dtype) for s in shapes]

    x4_shape = shape(3 * rows * SMALL, width)
    x0_shape = shape((rows + 2) * SMALL, width)
    d_shapes = [
        shape(3, *d_shape(BORDERS[0]).shape, dtype=BF16),
        shape(3, *d_shape(BORDERS[1]).shape, dtype=BF16),
        d_shape(EMPTY),
    ]
    planes = shape(2, 3 * rows, width)
    part = shape(2 * rows + SMALL, width)
    total = shape(pack_rows(ch), LANES)
    half = shape(pack_rows(ch) // 2, LANES)
    gh, x4, d3, d2, d1 = call(
        functools.partial(back_kernel, axis, rows, ch),
        [part, x4_shape] + d_shapes,
        [],
        (cotangent, pre_acts, m1_a, m1_b, w4, w3, w2, w1),
        {1: pre_spec(1)},
    )
    gh_a, gh_b = swap(gh, gh)
    before, u1, u0, x0s = call(
        functools.partial(term_kernel, axis, rows, ch),
        [total, planes, planes, x0_shape],
        scratch(x0_shape),
        (x4, d3, d2, d1, pre_acts, states, m0_a, m0_b),
        {4: pre_spec(1)},
    )
    keep, give, g, d1 = call(
        functools.partial(front_kernel, axis, rows, ch),
        [half, half, shape(2, rows, width), d_shapes[2]],
        scratch(x4_shape, d_shapes[0], d_shapes[1], total, planes),
        (gh, gh_a, gh_b, u1, x0s, pre_acts, m0_a, m0_b, w4, w3, w2, before),
        {5: pre_spec(0)},
    )
    gh0 = call(functools.partial(input_kernel, rows, ch), part, [], (g, d1, w1))
    gh0_a, gh0_b = swap(gh0, gh0)
    adjoint = call(
        functools.partial(last_kernel, axis, rows),
        shape(2, rows, width),
        scratch(planes),
        (gh0, gh0_a, gh0_b, u0),
    )

    mine = keep + lax.ppermute(give, axis, pair_a)
    bit = 2
    while bit < count:
        mine = mine.astype(BF16)
        steps = (bit, 2 * bit, 3 * bit) if 2 * bit < count else (bit,)
        got = []
        for b in steps:
            got.append(lax.ppermute(mine, axis, [(i, i ^ b) for i in range(count)]))
        bit *= len(steps) + 1
        if bit >= count:
            got, adjoint = lax.optimization_barrier((got, adjoint))
        terms = [t.astype(F32) for t in [mine] + got]
        sums = [a + b for a, b in zip(terms[::2], terms[1::2])]
        mine = sums[0] if len(sums) == 1 else sums[0] + sums[1]
    other = lax.ppermute(mine, axis, pair_a)
    factor = 1.0 / math.sqrt(rows * count * width)
    g1, g2, g3, g4 = call(
        functools.partial(unpack_kernel, axis, ch, factor),
        [
            shape(*w)
            for w in (
                weight_out.shape[:1] + (weight_in.shape[2], ch),
                weight_second.shape,
                weight_third.shape,
                weight_out.shape,
            )
        ],
        [],
        (mine, other),
    )
    return adjoint, jnp.swapaxes(g1, 1, 2), g2, g3, g4


def solution(mesh):
    return jax.shard_map(
        on_device,
        mesh=mesh,
        in_specs=(
            P(None, "groups", "gx", None),
            P(None, None, ("groups", "gx"), None, None),
            P("groups", "gx", None),
            P(),
            P(),
            P(),
            P(),
        ),
        out_specs=(
            P("groups", "gx", None),
            P("groups", None, None),
            P("groups", None, None),
            P("groups", None, None),
            P("groups", None, None),
        ),
        check_vma=False,
    )
```

```python
import functools
import math

import jax
import jax.numpy as jnp
from jax import lax
from jax.experimental import pallas as pl
from jax.experimental.pallas import tpu as pltpu
from jax.sharding import PartitionSpec as P


STEP = 0.25
VISC = 0.4
LANES = 128
BLOCK = 3
BLOCK4 = 4
VMEM_BYTES = 67043328
BORDERS = (2, 1, 0)
EMPTY = 2
SMALL = 8

F32 = jnp.float32
BF16 = jnp.bfloat16


def lane_roll(x, shift):
    width = x.shape[-1]
    return pltpu.roll(x, shift % width, x.ndim - 1)


def row_roll(x, shift):
    return pltpu.roll(x, shift % x.shape[0], 0)


def half_step(r, c):
    face = 0.25 * (r + row_roll(r, -1))
    side = 0.25 * (c + lane_roll(c, -1))
    outs = []
    for f in (r, c):
        down, right = row_roll(f, -1), lane_roll(f, -1)
        p = face * (f + down)
        q = side * (f + right)
        div = p - row_roll(p, 1) + (q - lane_roll(q, 1))
        lap = down + row_roll(f, 1) + right + lane_roll(f, 1) - 4.0 * f
        outs.append(f + STEP * (VISC * lap - div))
    return outs


def half_step_transpose(r, c, lr, lc):
    face = 0.25 * (r + row_roll(r, -1))
    side = 0.25 * (c + lane_roll(c, -1))
    outs = []
    extra_r = None
    extra_c = None
    for f, l in ((r, lr), (c, lc)):
        l_down, l_right = row_roll(l, -1), lane_roll(l, -1)
        a = STEP * (l_down - l)
        b = STEP * (l_right - l)
        ap, bq = a * face, b * side
        lap = l_down + row_roll(l, 1) + l_right + lane_roll(l, 1) - 4.0 * l
        outs.append(
            l + (STEP * VISC) * lap + (ap + row_roll(ap, 1)) + (bq + lane_roll(bq, 1))
        )
        af = a * (0.25 * (f + row_roll(f, -1)))
        bf = b * (0.25 * (f + lane_roll(f, -1)))
        extra_r = af if extra_r is None else extra_r + af
        extra_c = bf if extra_c is None else extra_c + bf
    return [
        outs[0] + (extra_r + row_roll(extra_r, 1)),
        outs[1] + (extra_c + lane_roll(extra_c, 1)),
    ]


def joined(a, own, b, even):
    return jnp.concatenate([jnp.where(even, b, a), own, jnp.where(even, a, b)], axis=0)


def split_terms(x):
    high = x.astype(BF16).astype(F32)
    return jnp.concatenate([high, x - high], axis=0).astype(BF16)


def border_planes(ref, first, rows, count):
    parts = [
        ref[first + 2 * rows * i : first + 2 * rows * (i + 1), :].astype(F32)
        for i in range(count)
    ]
    return [p[:rows] + p[rows:] for p in parts]


def fill_small(dst, planes, rows, row0, sign):
    dst[...] = jnp.zeros(dst.shape, F32)
    for comp, plane in enumerate(planes):
        value = plane.astype(BF16).astype(F32)
        for q in range(3):
            moved = value if q == 1 else lane_roll(value, sign * (q - 1))
            for i in range(rows):
                dst[SMALL * i + 2 * q + comp : SMALL * i + 2 * q + comp + 1, :] = moved[
                    row0 + i : row0 + i + 1, :
                ]


def row_conv(w_ref, src, src0, lo, hi, ch, emit):
    spare = w_ref.shape[1] // 3 - (BLOCK + 2) * ch
    row = lo
    while row < hi:
        start = min(row, hi - BLOCK)
        skip = row - start
        first = (start - 1 - src0) * ch
        parts = []
        for q in range(3):
            parts.append(src[q, first : first + (BLOCK + 2) * ch, :])
            if spare:
                parts.append(jnp.zeros((spare, src.shape[2]), BF16))
        y = jnp.dot(
            w_ref[skip * ch : BLOCK * ch, :],
            jnp.concatenate(parts, axis=0),
            preferred_element_type=F32,
        )
        for k in range(BLOCK - skip):
            emit(row + k, y[k * ch : (k + 1) * ch])
        row = start + BLOCK


def chain(x4, pre, m_a, m_b, even, w4, w3, w2, d3, d2, d1, rows, ch):
    e3, e2, e1 = BORDERS

    def mask_rows(layer, row):
        if rows <= row < 2 * rows:
            return pre[layer, row - rows]
        above = row < rows
        border, start = ((e1, e3 + e2), (e2, e3), (e3, 0))[layer]
        k = start + (row - (rows - border) if above else row - 2 * rows)
        a, b = (m[k * ch : (k + 1) * ch, :] for m in (m_a, m_b))
        return jnp.where(even, b, a) if above else jnp.where(even, a, b)

    def store(dst, layer, first):
        def emit(row, e):
            d = e.astype(BF16)
            d = jnp.where(mask_rows(layer, row) > 0, d, jnp.zeros_like(d))
            at = slice((row - first) * ch, (row - first + 1) * ch)
            if len(dst.shape) == 2:
                dst[at, :] = d
            else:
                for q in range(3):
                    dst[q, at, :] = lane_roll(d, q - 1) if q != 1 else d

        return emit

    row, emit = rows - e3, store(d3, 2, rows - e3)
    while row < 2 * rows + e3:
        count = min(BLOCK4, 2 * rows + e3 - row)
        rhs = x4[SMALL * (row - 1) : SMALL * (row + count + 1), :].astype(BF16)
        y = jnp.dot(
            w4[: count * ch, : SMALL * (count + 2)], rhs, preferred_element_type=F32
        )
        for k in range(count):
            emit(row + k, y[k * ch : (k + 1) * ch])
        row += count
    row_conv(w3, d3, rows - e3, rows - e2, 2 * rows + e2, ch, store(d2, 1, rows - e2))
    empty = jnp.zeros((EMPTY * ch, d1.shape[-1]), BF16)
    d1[: EMPTY * ch, :] = empty
    d1[(rows + EMPTY) * ch :, :] = empty
    row_conv(w2, d2, rows - e2, rows, 2 * rows, ch, store(d1, 0, rows - EMPTY))


def first_conv(w1, d1, src0, lo, hi, ch, emit):
    row = lo
    while row < hi:
        start = min(row, hi - BLOCK)
        rhs = d1[(start - 1 - src0) * ch : (start + BLOCK + 1 - src0) * ch, :]
        y = jnp.dot(w1[...], rhs, preferred_element_type=F32)
        e = (
            y[SMALL : 2 * SMALL]
            + lane_roll(y[:SMALL], -1)
            + lane_roll(y[2 * SMALL : 3 * SMALL], 1)
        )
        for k in range(row - start, BLOCK):
            emit(start + k, [e[2 * k + comp : 2 * k + comp + 1, :] for comp in range(2)])
        row = start + BLOCK


def weight_terms(x4, d3, d2, d1, pre, x0s, rows, ch):
    dims = (((1,), (1,)), ((), ()))

    def product(a, b):
        return lax.dot_general(a, b, dims, preferred_element_type=F32)

    def three(ref, row, border):
        row -= rows - border
        return ref[1, (row - 1) * ch : (row + 2) * ch, :]

    def lanes(values):
        return jnp.concatenate(list(values), axis=1)

    def source(layer, i):
        a = pre[layer, i]
        return jnp.maximum(a, jnp.zeros_like(a))

    def moved(layer, i):
        h = source(layer, i)
        return jnp.concatenate([lane_roll(h, 1), h, lane_roll(h, -1)], axis=0)

    each = range(rows)
    return (
        product(
            lanes(x0s[SMALL * i : SMALL * (i + 3), :].astype(BF16) for i in each),
            lanes(d1[(i + EMPTY) * ch : (i + EMPTY + 1) * ch, :] for i in each),
        ),
        product(
            lanes(three(d2, rows + i, BORDERS[1]) for i in each),
            lanes(moved(0, i) for i in each),
        ),
        product(
            lanes(three(d3, rows + i, BORDERS[0]) for i in each),
            lanes(moved(1, i) for i in each),
        ),
        product(
            lanes(
                x4[SMALL * (rows + i - 1) : SMALL * (rows + i + 2), :].astype(BF16)
                for i in each
            ),
            lanes(source(2, i) for i in each),
        ),
    )


def pack_rows(ch):
    n = 3 * ch
    return -(-(2 * n + n // 2 + 3 * SMALL) // 32) * 32


def pack_terms(t_ref, terms, ch, before=None):
    g1, g2, g3, g4 = terms
    n = 3 * ch
    low = 2 * n + n // 2
    tail = jnp.concatenate([g2[:, LANES:], g3[:, LANES:]], axis=1)
    wide = tail.shape[1]
    parts = (
        (0, n, 0, LANES, g2[:, :LANES]),
        (n, 2 * n, 0, LANES, g3[:, :LANES]),
        (2 * n, low, 0, wide, tail[: n // 2]),
        (2 * n, low, wide, 2 * wide, tail[n // 2 :]),
        (low, low + 3 * SMALL, 0, 2 * ch, jnp.concatenate([g4, g1], axis=1)),
    )
    t_ref[2 * n :, :] = jnp.zeros((t_ref.shape[0] - 2 * n, LANES), F32)
    for r0, r1, c0, c1, value in parts:
        if before is not None:
            value = value + before[r0:r1, c0:c1]
        t_ref[r0:r1, c0:c1] = value


def gather_kernel(axis, takes, rows, ch, base, step, late, pre_hbm, more, out_a, out_b, sems, buf):
    even = lax.rem(lax.axis_index(axis), 2) == 0
    copies = [pltpu.make_async_copy(more, buf, sems.at[0])]
    for layer, count, dst in takes:
        low, high = 0, (rows - count) * ch
        for out, start in (
            (out_a, jnp.where(even, high, low)),
            (out_b, jnp.where(even, low, high)),
        ):
            copies.append(
                pltpu.make_async_copy(
                    pre_hbm.at[step, layer, pl.ds(pl.multiple_of(start, ch), count * ch)],
                    out.at[pl.ds(dst * ch, count * ch)],
                    sems.at[len(copies)],
                )
            )
    for copy in copies:
        copy.start()
    copies[0].wait()
    if late:
        planes = [split_terms(buf[k, comp]) for k in range(2) for comp in range(2)]
    else:
        planes = [jnp.concatenate([buf[0], buf[1]], axis=0).astype(BF16)]
    for i, plane in enumerate(planes):
        for out in (out_a, out_b):
            out[base + 2 * rows * i : base + 2 * rows * (i + 1), :] = plane
    for copy in copies[1:]:
        copy.wait()


def weights_kernel(ch, w1, w2, w3, w4, o1, o2, o3, o4):
    for w, o in ((w3, o3), (w2, o2)):
        wide = o.shape[1] // 3
        for q in range(3):
            block = jnp.concatenate([w[3 * (2 - m) + q].astype(F32) for m in range(3)], axis=0)
            block = block.T.astype(BF16)
            for b in range(BLOCK):
                o[b * ch : (b + 1) * ch, q * wide : (q + 1) * wide] = placed(block, b * ch, wide)
    zero = jnp.zeros((SMALL - 6, ch), F32)
    block = jnp.concatenate(
        [
            piece
            for m in range(3)
            for piece in [w4[3 * (2 - m) + q].astype(F32) for q in range(3)] + [zero]
        ],
        axis=0,
    )
    block = block.T.astype(BF16)
    for b in range(BLOCK4):
        o4[b * ch : (b + 1) * ch, :] = placed(block, b * SMALL, o4.shape[1])
    rows = []
    for q in range(3):
        block = jnp.concatenate([w1[3 * (2 - m) + q].astype(F32) for m in range(3)], axis=1)
        for b in range(BLOCK):
            rows.append(placed(block, b * ch, o1.shape[1]))
        rows.append(jnp.zeros((SMALL - 2 * BLOCK, o1.shape[1]), F32))
    o1[...] = jnp.concatenate(rows, axis=0).astype(BF16)


def placed(block, column, width):
    parts = [block]
    if column:
        parts.insert(0, jnp.zeros((block.shape[0], column), block.dtype))
    rest = width - column - block.shape[1]
    if rest:
        parts.append(jnp.zeros((block.shape[0], rest), block.dtype))
    return jnp.concatenate(parts, axis=1)


def partial_input(w1, d1, own, out, rows, ch):
    out[2 * rows :, :] = jnp.zeros((SMALL, out.shape[1]), F32)

    def emit(row, values):
        i = row - rows
        for comp in range(2):
            if 0 <= i < rows:
                k = rows * comp + i
                out[k : k + 1, :] = own(comp, i) + values[comp]
            else:
                k = 2 * rows + 2 * comp + (i > 0)
                out[k : k + 1, :] = values[comp]

    first_conv(w1, d1, rows - EMPTY, rows - 1, 2 * rows + 1, ch, emit)


def whole_input(gh, gh_a, gh_b, lam, rows, even):
    a, b = gh_a[...], gh_b[...]
    above, below = jnp.where(even, b, a), jnp.where(even, a, b)
    for comp in range(2):
        own = slice(rows * comp, rows * (comp + 1))
        lam[comp, :rows, :] = above[own]
        lam[comp, rows : 2 * rows, :] = gh[own, :]
        lam[comp, 2 * rows :, :] = below[own]
        k = 2 * rows + 2 * comp
        for row, part in (
            (rows - 1, gh[k : k + 1, :]),
            (rows, above[k + 1 : k + 2]),
            (2 * rows - 1, below[k : k + 1]),
            (2 * rows, gh[k + 1 : k + 2, :]),
        ):
            lam[comp, row : row + 1, :] += part


def border_states(states, step, m_a, m_b, rows, ch, even):
    first = sum(BORDERS) * ch + 4 * rows * step
    a = border_planes(m_a, first, rows, 2)
    b = border_planes(m_b, first, rows, 2)
    return [joined(a[comp], states[step, comp], b[comp], even) for comp in range(2)]


def back_kernel(axis, rows, ch, cot, pre, m_a, m_b, w4, w3, w2, w1, gh, x4, d3, d2, d1):
    even = lax.rem(lax.axis_index(axis), 2) == 0
    base = sum(BORDERS) * ch
    a, b = (m[base : base + 2 * rows, :].astype(F32) for m in (m_a, m_b))
    planes = [
        joined(
            a[rows * comp : rows * (comp + 1)], cot[comp], b[rows * comp : rows * (comp + 1)], even
        )
        for comp in range(2)
    ]
    fill_small(x4, planes, 3 * rows, 0, 1)
    chain(x4, pre.at[0], m_a, m_b, even, w4, w3, w2, d3, d2, d1, rows, ch)
    partial_input(w1, d1, lambda comp, i: cot[comp, i : i + 1, :], gh, rows, ch)


def term_kernel(
    axis, rows, ch,
    x4, d3, d2, d1, pre, states, m_a, m_b,
    t_out, u1, u0, x0s, x1s,
):
    even = lax.rem(lax.axis_index(axis), 2) == 0
    for step, out, small in ((1, u1, x1s), (0, u0, x0s)):
        u = border_states(states, step, m_a, m_b, rows, ch, even)
        for comp in range(2):
            out[comp] = u[comp]
        fill_small(small, half_step(*u), rows + 2, rows - 1, -1)
    pack_terms(t_out, weight_terms(x4, d3, d2, d1, pre.at[0], x1s, rows, ch), ch)


def front_kernel(
    axis, rows, ch,
    gh, gh_a, gh_b, u1, x0s, pre, m_a, m_b, w4, w3, w2, before,
    keep, give, g_out, d1, x4, d3, d2, total, lam,
):
    even = lax.rem(lax.axis_index(axis), 2) == 0
    whole_input(gh, gh_a, gh_b, lam, rows, even)
    planes = half_step_transpose(u1[0], u1[1], lam[0], lam[1])
    for comp in range(2):
        g_out[comp] = planes[comp][rows : 2 * rows]
    fill_small(x4, planes, 3 * rows, 0, 1)
    chain(x4, pre.at[0], m_a, m_b, even, w4, w3, w2, d3, d2, d1, rows, ch)
    pack_terms(total, weight_terms(x4, d3, d2, d1, pre.at[0], x0s, rows, ch), ch, before)
    half = total.shape[0] // 2
    a, b = total[:half, :], total[half:, :]
    keep[...] = jnp.where(even, a, b)
    give[...] = jnp.where(even, b, a).astype(BF16)


def input_kernel(rows, ch, g, d1, w1, gh):
    partial_input(w1, d1, lambda comp, i: g[comp, i : i + 1, :], gh, rows, ch)


def last_kernel(axis, rows, gh, gh_a, gh_b, u, out, lam):
    even = lax.rem(lax.axis_index(axis), 2) == 0
    whole_input(gh, gh_a, gh_b, lam, rows, even)
    planes = half_step_transpose(u[0], u[1], lam[0], lam[1])
    for comp in range(2):
        out[comp] = planes[comp][rows : 2 * rows]


def unpack_kernel(axis, ch, factor, mine, other, o1, o2, o3, o4):
    even = lax.rem(lax.axis_index(axis), 2) == 0
    a, b = mine[...].astype(F32), other[...].astype(F32)
    t = factor * jnp.concatenate([jnp.where(even, a, b), jnp.where(even, b, a)], axis=0)
    n = 3 * ch
    rest = n - LANES
    wide = 2 * rest
    low = 2 * n + n // 2
    tail = t[2 * n : low]
    tail = jnp.concatenate([tail[:, :wide], tail[:, wide : 2 * wide]], axis=0)
    g2 = jnp.concatenate([t[:n], tail[:, :rest]], axis=1)
    g3 = jnp.concatenate([t[n : 2 * n], tail[:, rest:]], axis=1)
    g4 = t[low : low + 3 * SMALL, :ch]
    g1 = t[low : low + 3 * SMALL, ch : 2 * ch]
    for m in range(3):
        for q in range(3):
            tap = 3 * (2 - m) + q
            o2[tap] = g2[m * ch : (m + 1) * ch, q * ch : (q + 1) * ch]
            o3[tap] = g3[m * ch : (m + 1) * ch, q * ch : (q + 1) * ch]
            small = slice(m * SMALL + 2 * q, m * SMALL + 2 * q + 2)
            o4[tap] = g4[small]
            o1[3 * m + q] = g1[small]


VMEM = pl.BlockSpec(memory_space=pltpu.VMEM)


def call(kernel, outs, scratch, args, specs=None, limit=24 << 20, flops=10**8):
    specs = specs or {}
    return pl.pallas_call(
        kernel,
        out_shape=outs,
        grid=(1,) if specs else (),
        in_specs=[specs.get(i, VMEM) for i in range(len(args))],
        out_specs=jax.tree.map(lambda _: VMEM, outs),
        scratch_shapes=scratch,
        compiler_params=pltpu.CompilerParams(vmem_limit_bytes=limit),
        cost_estimate=pl.CostEstimate(
            flops=flops, bytes_accessed=2 * 10**6, transcendentals=0
        ),
    )(*args)


def on_device(states, pre_acts, cotangent, weight_in, weight_second, weight_third, weight_out):
    axis = "gx"
    count = lax.axis_size(axis)
    _, _, rows, width = states.shape
    ch = pre_acts.shape[3]
    flat = pre_acts.reshape(pre_acts.shape[:2] + (rows * ch, width))

    pair_a = [(i, i ^ 1) for i in range(count)]
    pair_b = [(i, (i + 1) % count if i % 2 else (i - 1) % count) for i in range(count)]

    def swap(for_a, for_b):
        b = lax.ppermute(for_b, axis, pair_b)
        a = lax.ppermute(for_a, axis, pair_a)
        return a, b

    def shape(*dims, dtype=F32):
        return jax.ShapeDtypeStruct(dims, dtype)

    def borders(step, late, room):
        takes, total = [], 0
        for layer, border in zip((2, 1, 0), BORDERS):
            if not border:
                continue
            takes.append((layer, border, total))
            total += border
        base = total * ch
        more = states if late else cotangent
        out = shape(base + 2 * rows * (4 if late else 1), width, dtype=BF16)
        pack = pl.pallas_call(
            functools.partial(gather_kernel, axis, takes, rows, ch, base, step, late),
            out_shape=[out, out],
            in_specs=[pl.BlockSpec(memory_space=pltpu.HBM)] * 2,
            out_specs=[VMEM, VMEM],
            scratch_shapes=[
                pltpu.SemaphoreType.DMA((2 * len(takes) + 1,)),
                pltpu.VMEM(more.shape, F32),
            ],
            compiler_params=pltpu.CompilerParams(vmem_limit_bytes=VMEM_BYTES - room),
        )
        a, b = pack(flat, more)
        return swap(a, b)

    m1_a, m1_b = borders(1, False, 3 << 20)
    m0_a, m0_b = borders(0, True, 56 << 20)

    def bands(n, m):
        return shape(n, m, dtype=BF16)

    wide = -(-(BLOCK + 2) * ch // LANES) * LANES
    w1, w2, w3, w4 = call(
        functools.partial(weights_kernel, ch),
        [
            bands(3 * SMALL, (BLOCK + 2) * ch),
            bands(BLOCK * ch, 3 * wide),
            bands(BLOCK * ch, 3 * wide),
            bands(BLOCK4 * ch, (BLOCK4 + 2) * SMALL),
        ],
        [],
        (jnp.swapaxes(weight_in, 1, 2), weight_second, weight_third, weight_out),
    )

    def pre_spec(step):
        return pl.BlockSpec((1,) + pre_acts.shape[1:], lambda *_: (step, 0, 0, 0, 0))

    def d_shape(border):
        return shape((rows + 2 * border) * ch, width, dtype=BF16)

    def scratch(*shapes):
        return [pltpu.VMEM(s.shape, s.dtype) for s in shapes]

    x4_shape = shape(3 * rows * SMALL, width)
    x0_shape = shape((rows + 2) * SMALL, width)
    d_shapes = [
        shape(3, *d_shape(BORDERS[0]).shape, dtype=BF16),
        shape(3, *d_shape(BORDERS[1]).shape, dtype=BF16),
        d_shape(EMPTY),
    ]
    planes = shape(2, 3 * rows, width)
    part = shape(2 * rows + SMALL, width)
    total = shape(pack_rows(ch), LANES)
    half = shape(pack_rows(ch) // 2, LANES)
    gh, x4, d3, d2, d1 = call(
        functools.partial(back_kernel, axis, rows, ch),
        [part, x4_shape] + d_shapes,
        [],
        (cotangent, pre_acts, m1_a, m1_b, w4, w3, w2, w1),
        {1: pre_spec(1)},
    )
    gh_a, gh_b = swap(gh, gh)
    before, u1, u0, x0s = call(
        functools.partial(term_kernel, axis, rows, ch),
        [total, planes, planes, x0_shape],
        scratch(x0_shape),
        (x4, d3, d2, d1, pre_acts, states, m0_a, m0_b),
        {4: pre_spec(1)},
    )
    keep, give, g, d1 = call(
        functools.partial(front_kernel, axis, rows, ch),
        [half, shape(*half.shape, dtype=BF16), shape(2, rows, width), d_shapes[2]],
        scratch(x4_shape, d_shapes[0], d_shapes[1], total, planes),
        (gh, gh_a, gh_b, u1, x0s, pre_acts, m0_a, m0_b, w4, w3, w2, before),
        {5: pre_spec(0)},
    )
    gh0 = call(functools.partial(input_kernel, rows, ch), part, [], (g, d1, w1))
    gh0_a, gh0_b = swap(gh0, gh0)
    adjoint = call(
        functools.partial(last_kernel, axis, rows),
        shape(2, rows, width),
        scratch(planes),
        (gh0, gh0_a, gh0_b, u0),
    )

    mine = keep + lax.ppermute(give, axis, pair_a).astype(F32)
    bit = 2
    while bit < count:
        mine = mine.astype(BF16)
        steps = (bit, 2 * bit, 3 * bit) if 2 * bit < count else (bit,)
        got = []
        for b in steps:
            got.append(lax.ppermute(mine, axis, [(i, i ^ b) for i in range(count)]))
        bit *= len(steps) + 1
        if bit >= count:
            got, adjoint = lax.optimization_barrier((got, adjoint))
        terms = [t.astype(F32) for t in [mine] + got]
        sums = [a + b for a, b in zip(terms[::2], terms[1::2])]
        mine = sums[0] if len(sums) == 1 else sums[0] + sums[1]
    other = lax.ppermute(mine, axis, pair_a)
    factor = 1.0 / math.sqrt(rows * count * width)
    g1, g2, g3, g4 = call(
        functools.partial(unpack_kernel, axis, ch, factor),
        [
            shape(*w)
            for w in (
                weight_out.shape[:1] + (weight_in.shape[2], ch),
                weight_second.shape,
                weight_third.shape,
                weight_out.shape,
            )
        ],
        [],
        (mine, other),
    )
    return adjoint, jnp.swapaxes(g1, 1, 2), g2, g3, g4


def solution(mesh):
    return jax.shard_map(
        on_device,
        mesh=mesh,
        in_specs=(
            P(None, "groups", "gx", None),
            P(None, None, ("groups", "gx"), None, None),
            P("groups", "gx", None),
            P(),
            P(),
            P(),
            P(),
        ),
        out_specs=(
            P("groups", "gx", None),
            P("groups", None, None),
            P("groups", None, None),
            P("groups", None, None),
            P("groups", None, None),
        ),
        check_vma=False,
    )
```
